128 devices in a mesh: layer: 4 (over y_hi, core), tensor: 32 (over z, x, y_lo).
Axes of the slice: x: 4, y: 4 (y_hi: 2, y_lo: 2; y = y_hi * 2 + y_lo), z: 4, core: 2. Of those that a mesh axis runs over, the one named last changes fastest.
Arguments:
- weight_slab: bfloat16 [32768, 8192], P(('layer', 'tensor')), parts along dimension 0, may hold values from -0.0625 to 0.0625
- token_rows: bfloat16 [4096, 8192], P(('layer', 'tensor')), parts along dimension 0, may hold values from -6 to 6
- skew_params: float32 [24, 64, 128, 128], P('layer', 'tensor'), parts along dimension 0, may hold values from -0.2 to 0.2
- pairing: int32 [24, 128], P('layer'), parts along dimension 0, may hold values from 0 to 127, each once within a row
Outputs:
- projected: bfloat16 [4096, 8192], P(('layer', 'tensor')), parts along dimension 0
The draws below stay inside these ranges and needn't reach their ends.
There are 4 independent parts, one for each index of `layer`. The reference program is written for one: setup_inputs(seed, part) draws one part's arguments, and reference() takes and returns one part's arrays. A program takes and returns all parts, laid end to end along the dimension named above; each array names one. Nothing has to cross between parts.
Inputs may be any that keep to these rules, and one draw needn't show every extreme that they name: Each row of pairing is a permutation of 0 to 127.
All inputs are finite; a program needn't handle non-finite values.
Results may differ from the reference program's by a relative error of at most 0.025.
Values may be sent and summed in bfloat16 or wider, within the bound.
A program may use at most 128 MiB of HBM per device.

```python
import jax
import jax.numpy as jnp
import numpy as np
from jax import lax

D = 8192
COLS = 8192
BLOCK = 128
SECTIONS = 6
TOKENS = 1024
BLOCKS = 64
N_TENSOR = 32


def levels(rng, dims, pieces, smallest, top_value):
    gain, own = 1.0, jax.random.fold_in(rng, 6)
    for axis_at, parts in pieces:
        draws = jnp.exp(jax.random.uniform(jax.random.fold_in(own, axis_at), (parts,), jnp.float32, smallest / len(pieces), top_value / len(pieces)))
        gain = gain * jnp.repeat(draws, dims[axis_at] // parts).reshape([-1 if axis == axis_at else 1 for axis in range(len(dims))])
    return gain


def noise(rng, shape, spread, most, shards=(), kind=jnp.bfloat16):
    values = jax.random.normal(rng, shape, jnp.float32) * spread
    if len(shards) > 0:
        values = levels(rng, shape, shards, -0.22, 0.18) * values
    return jnp.clip(values, min=-most, max=most).astype(kind)


def setup_inputs(seed: int = 0, part: int = 0) -> dict:
    key_list = jax.random.split(jax.random.key(seed), 5)
    part_keys = jax.random.split(jax.random.fold_in(key_list[4], part), 5)
    weight_slab = noise(part_keys[0], (D, COLS), D ** -0.5, 0.0625, ((0, 32),))
    token_rows = noise(part_keys[1], (TOKENS, D), 1.0, 6.0, ((0, 32),))
    skew_params = noise(part_keys[2], (SECTIONS, BLOCKS, BLOCK, BLOCK), 0.03, 0.2, ((1, 32),), jnp.float32)
    pairing = jax.vmap(lambda own: jax.random.permutation(own, BLOCK))(jax.random.split(part_keys[3], SECTIONS)).reshape((SECTIONS, BLOCK)).astype(jnp.int32)
    return {"weight_slab": weight_slab, "token_rows": token_rows, "skew_params": skew_params, "pairing": pairing}


section_bits = (0, 2, 3, 4, 5, 6)

def pair_table(distance, count):
    stride = 1 << distance
    groups = count // (2 * stride)
    lookup = np.zeros((groups, stride), np.int32)
    for group_idx in range(groups):
        for offset in range(stride):
            lower_half = group_idx * 2 * stride + offset
            member = lower_half if lower_half >> 1 & 1 == 0 else lower_half + stride
            lookup[group_idx, offset] = (member >> 2) * 2 + (member & 1)
    return lookup

def chol_solve(factor, target):
    first = lax.linalg.triangular_solve(factor, target, left_side=True, lower=True)
    return lax.linalg.triangular_solve(factor, first, left_side=True, lower=True, transpose_a=True)

def cayley_blocks(skew_part, order_row):
    block_len = skew_part.shape[-1]
    identity = jnp.eye(block_len, dtype=jnp.float32)
    chosen = (order_row[:, None] == jnp.arange(block_len, dtype=jnp.int32)[None, :]).astype(jnp.float32)

    def one_block(params):
        skewed = params - params.T
        square = jnp.dot(skewed, skewed, precision=lax.Precision.HIGHEST)
        factor = jnp.linalg.cholesky(identity - square)
        raised = identity + skewed
        rotation = chol_solve(factor, jnp.dot(raised, raised, precision=lax.Precision.HIGHEST))
        inner = jnp.dot(rotation, chosen, precision=lax.Precision.HIGHEST)
        return jnp.dot(chosen.T, inner, precision=lax.Precision.HIGHEST)
    return lax.map(one_block, skew_part).astype(jnp.bfloat16)

def reference(weight_slab, token_rows, skew_params, pairing):
    half_len = BLOCK // 2
    count = D // half_len
    current = weight_slab
    for section_idx in range(SECTIONS):
        distance = section_bits[section_idx]
        rotations = cayley_blocks(skew_params[section_idx], pairing[section_idx])
        lookup = pair_table(distance, count)
        picked = rotations[lookup.reshape(-1)].astype(jnp.float32)
        groups = count >> distance + 1
        stride = 1 << distance
        grouped = current.reshape(groups, 2, stride, half_len, COLS)
        joined = jnp.concatenate([grouped[:, 0], grouped[:, 1]], axis=2).reshape(groups * stride, BLOCK, COLS)
        rotated = jnp.einsum('kij,kjn->kin', picked, joined.astype(jnp.float32)).astype(jnp.bfloat16)
        rotated = rotated.reshape(groups, stride, 2, half_len, COLS)
        current = jnp.stack([rotated[:, :, 0], rotated[:, :, 1]], axis=1).reshape(D, COLS)
    shard = D // N_TENSOR

    def add_part(total, index):
        slab_rows = lax.dynamic_slice_in_dim(current, index * shard, shard, 0)
        token_cols = lax.dynamic_slice_in_dim(token_rows, index * shard, shard, 1)
        partial_term = jnp.dot(token_cols.astype(jnp.float32), slab_rows.astype(jnp.float32), preferred_element_type=jnp.float32).astype(jnp.bfloat16)
        partial_term = lax.optimization_barrier(partial_term)
        return (total + partial_term.astype(jnp.float32), None)
    start_total = jnp.zeros((TOKENS, COLS), jnp.float32)
    total, _ = lax.scan(add_part, start_total, jnp.arange(N_TENSOR, dtype=jnp.int32))
    return total.astype(jnp.bfloat16)
```

```python
import jax
import jax.numpy as jnp
import numpy as np
from jax import lax
from jax.experimental import pallas as pl
from jax.experimental.pallas import tpu as pltpu
from jax.sharding import PartitionSpec as P

HALF = 64
BLK = 128


def pair_table(distance, count):
    stride = 1 << distance
    rows = []
    for group in range(count // (2 * stride)):
        for offset in range(stride):
            low = group * 2 * stride + offset
            member = low if low >> 1 & 1 == 0 else low + stride
            rows.append((low, low + stride, (member >> 2) * 2 + (member & 1)))
    return rows


def rotation_kernel(skew_ref, pairing_ref, out_ref, work):
    count = work.shape[0]
    for block in range(count):
        raw = skew_ref[block]
        work[block] = raw.T - raw
    lanes = lax.broadcasted_iota(jnp.int32, (BLK, BLK), 1)
    lane_row = lax.broadcasted_iota(jnp.int32, (1, BLK), 1)

    def eliminate(step, carry):
        is_pivot = lanes == step
        pick = jnp.full((BLK, BLK), step, jnp.int32)
        unit = (lane_row == step).astype(jnp.float32)
        for block in range(count):
            current = work[block]
            column = jnp.take_along_axis(current, pick, axis=1)
            row = work[block, pl.ds(step, 1), :]
            pivot = 1.0 + jnp.sum(row * unit, axis=1, keepdims=True)
            scaled = (row * (1.0 - unit) + unit) / pivot
            work[block] = jnp.where(is_pivot, 0.0, current) - column * scaled
        return carry

    lax.fori_loop(0, BLK, eliminate, 0)
    rows = lax.broadcasted_iota(jnp.int32, (BLK, BLK), 0)
    identity = (rows == lanes).astype(jnp.float32)
    for block in range(count):
        order = pairing_ref[pl.ds(block // 2, 1), :]
        chosen = (rows == order).astype(jnp.bfloat16)
        rotation = (identity + 2.0 * work[block]).astype(jnp.bfloat16)
        inner = jnp.dot(chosen, rotation, preferred_element_type=jnp.float32).astype(jnp.bfloat16)
        outer = lax.dot_general(inner, chosen, (((1,), (1,)), ((), ())), preferred_element_type=jnp.float32)
        out_ref[block] = outer.astype(jnp.bfloat16)


def cayley_blocks(skew_params, pairing):
    sections, owned = skew_params.shape[:2]
    count = sections * owned
    out = pl.pallas_call(
        rotation_kernel,
        out_shape=jax.ShapeDtypeStruct((count, BLK, BLK), jnp.bfloat16),
        in_specs=[pl.BlockSpec(memory_space=pltpu.VMEM)] * 2,
        out_specs=pl.BlockSpec(memory_space=pltpu.VMEM),
        scratch_shapes=[pltpu.VMEM((count, BLK, BLK), jnp.float32)],
        cost_estimate=pl.CostEstimate(flops=count * BLK**3 * 20, bytes_accessed=count * BLK * BLK * 6, transcendentals=0),
    )(skew_params.reshape(count, BLK, BLK), pairing)
    return out.reshape(sections, owned, BLK, BLK)


def rotate_rows(slab, rotations, distance):
    halves = slab.shape[0] // HALF
    parts = [None] * halves
    for low, high, owner in pair_table(distance, halves):
        joined = jnp.concatenate([slab[low * HALF:(low + 1) * HALF], slab[high * HALF:(high + 1) * HALF]], axis=0)
        turned = jnp.dot(rotations[owner], joined, preferred_element_type=jnp.float32).astype(jnp.bfloat16)
        parts[low], parts[high] = turned[:HALF], turned[HALF:]
    return jnp.concatenate(parts, axis=0)


def rotate_cols(rows, rotations, distance):
    halves = rows.shape[1] // HALF
    parts = [None] * halves
    for low, high, owner in pair_table(distance, halves):
        joined = jnp.concatenate([rows[:, low * HALF:(low + 1) * HALF], rows[:, high * HALF:(high + 1) * HALF]], axis=1)
        turned = jnp.dot(joined, rotations[owner], preferred_element_type=jnp.float32).astype(jnp.bfloat16)
        parts[low], parts[high] = turned[:, :HALF], turned[:, HALF:]
    return jnp.concatenate(parts, axis=1)


def shards(weight_slab, token_rows, skew_params, pairing):
    plane = [[z * 8 + c for c in range(8)] for z in range(4)]
    column = [[z * 8 + c for z in range(4)] for c in range(8)]
    rotations = cayley_blocks(skew_params, pairing)
    slab = lax.all_to_all(weight_slab, "tensor", split_axis=1, concat_axis=0, axis_index_groups=plane, tiled=True)
    local = token_rows.reshape(32, 4, 8, 256)
    spread = lax.all_to_all(local, "tensor", split_axis=2, concat_axis=0, axis_index_groups=plane, tiled=True)
    spread = spread.reshape(256, 1024)
    rot_z = lax.all_gather(rotations[4:], "tensor", axis_index_groups=column, axis=1, tiled=True)
    rot_xy = lax.all_gather(rotations[:4], "tensor", axis_index_groups=plane, axis=1, tiled=True)
    spread = rotate_cols(spread, rot_z[1], 3)
    spread = rotate_cols(spread, rot_z[0], 2)
    features = lax.all_to_all(spread, "tensor", split_axis=1, concat_axis=0, axis_index_groups=column, tiled=True)
    features = lax.all_gather(features, "tensor", axis_index_groups=plane, axis=0)
    for section, distance in enumerate((0, 2, 3, 4)):
        slab = rotate_rows(slab, rot_xy[section], distance)
    partial = jnp.einsum("ptf,pfn->tn", features, slab.reshape(8, 256, 1024), preferred_element_type=jnp.float32)
    partial = partial.astype(jnp.bfloat16)
    landed = lax.all_to_all(partial, "tensor", split_axis=0, concat_axis=0, tiled=True)
    landed = landed.reshape(4, 8, 32, 1024).astype(jnp.float32).sum(axis=0)
    return landed.transpose(1, 0, 2).reshape(32, 8192).astype(jnp.bfloat16)


def solution(mesh):
    in_specs = (
        P(("layer", "tensor"), None),
        P(("layer", "tensor"), None),
        P("layer", "tensor", None, None),
        P("layer", None),
    )
    out_specs = P(("layer", "tensor"), None)
    return jax.shard_map(shards, mesh=mesh, in_specs=in_specs, out_specs=out_specs, check_vma=False)
```

```python
import jax
import jax.numpy as jnp
import numpy as np
from jax import lax
from jax.experimental import pallas as pl
from jax.experimental.pallas import tpu as pltpu
from jax.sharding import PartitionSpec as P

HALF = 64
BLK = 128


def pair_table(distance, count):
    stride = 1 << distance
    rows = []
    for group in range(count // (2 * stride)):
        for offset in range(stride):
            low = group * 2 * stride + offset
            member = low if low >> 1 & 1 == 0 else low + stride
            rows.append((low, low + stride, (member >> 2) * 2 + (member & 1)))
    return rows


def split_dot(left, right):
    left_hi = left.astype(jnp.bfloat16)
    left_lo = (left - left_hi.astype(jnp.float32)).astype(jnp.bfloat16)
    right_hi = right.astype(jnp.bfloat16)
    right_lo = (right - right_hi.astype(jnp.float32)).astype(jnp.bfloat16)
    return jnp.dot(
        jnp.concatenate([left_hi, left_hi, left_lo], axis=1),
        jnp.concatenate([right_hi, right_lo, right_hi], axis=0),
        preferred_element_type=jnp.float32,
    )


def full_dot(left, right):
    return jnp.dot(left, right, precision=lax.Precision.HIGHEST, preferred_element_type=jnp.float32)


def rotation_kernel(skew_ref, pairing_ref, out_ref, gram, guess):
    count = gram.shape[0]
    rows = lax.broadcasted_iota(jnp.int32, (BLK, BLK), 0)
    lanes = lax.broadcasted_iota(jnp.int32, (BLK, BLK), 1)
    identity = (rows == lanes).astype(jnp.float32)
    largest = jnp.zeros((1, BLK), jnp.float32)
    for block in range(count):
        raw = skew_ref[block]
        skewed = raw - raw.T
        square = full_dot(skewed, skewed)
        gram[block] = identity - square
        largest = jnp.maximum(largest, jnp.sum(square * square, axis=0, keepdims=True).sum(axis=1, keepdims=True))
    top = 1.0 + jnp.sqrt(0.5 * jnp.max(largest)) * 1.0001
    start = 2.0 / (1.0 + top)
    for block in range(count):
        guess[block] = identity * start

    def more(state):
        return state > 2e-2

    def improve(spread):
        shrunk = spread * spread / (2.0 - spread * spread)
        scale = 2.0 / (2.0 - spread * spread)
        for block in range(count):
            now = guess[block]
            left = 2.0 * identity - split_dot(gram[block], now)
            guess[block] = scale * split_dot(now, left)
        return shrunk

    lax.while_loop(more, improve, (top - 1.0) / (top + 1.0))
    for block in range(count):
        raw = skew_ref[block]
        raised = identity + raw - raw.T
        now = guess[block]
        now = now + split_dot(now, identity - full_dot(gram[block], now))
        rotation = (2.0 * full_dot(now, raised) - identity).astype(jnp.bfloat16)
        order = pairing_ref[pl.ds(block // 2, 1), :]
        chosen = (rows == order).astype(jnp.bfloat16)
        inner = jnp.dot(chosen, rotation, preferred_element_type=jnp.float32).astype(jnp.bfloat16)
        outer = lax.dot_general(inner, chosen, (((1,), (1,)), ((), ())), preferred_element_type=jnp.float32)
        out_ref[block] = outer.astype(jnp.bfloat16)


def cayley_blocks(skew_params, pairing):
    sections, owned = skew_params.shape[:2]
    count = sections * owned
    out = pl.pallas_call(
        rotation_kernel,
        out_shape=jax.ShapeDtypeStruct((count, BLK, BLK), jnp.bfloat16),
        in_specs=[pl.BlockSpec(memory_space=pltpu.VMEM)] * 2,
        out_specs=pl.BlockSpec(memory_space=pltpu.VMEM),
        scratch_shapes=[pltpu.VMEM((count, BLK, BLK), jnp.float32)] * 2,
        cost_estimate=pl.CostEstimate(flops=count * BLK**3 * 20, bytes_accessed=count * BLK * BLK * 6, transcendentals=0),
    )(skew_params.reshape(count, BLK, BLK), pairing)
    return out.reshape(sections, owned, BLK, BLK)


def rotate_rows(slab, rotations, distance):
    halves = slab.shape[0] // HALF
    parts = [None] * halves
    for low, high, owner in pair_table(distance, halves):
        joined = jnp.concatenate([slab[low * HALF:(low + 1) * HALF], slab[high * HALF:(high + 1) * HALF]], axis=0)
        turned = jnp.dot(rotations[owner], joined, preferred_element_type=jnp.float32).astype(jnp.bfloat16)
        parts[low], parts[high] = turned[:HALF], turned[HALF:]
    return jnp.concatenate(parts, axis=0)


def rotate_cols(rows, rotations, distance):
    halves = rows.shape[1] // HALF
    parts = [None] * halves
    for low, high, owner in pair_table(distance, halves):
        joined = jnp.concatenate([rows[:, low * HALF:(low + 1) * HALF], rows[:, high * HALF:(high + 1) * HALF]], axis=1)
        turned = jnp.dot(joined, rotations[owner], preferred_element_type=jnp.float32).astype(jnp.bfloat16)
        parts[low], parts[high] = turned[:, :HALF], turned[:, HALF:]
    return jnp.concatenate(parts, axis=1)


def shards(weight_slab, token_rows, skew_params, pairing):
    plane = [[z * 8 + c for c in range(8)] for z in range(4)]
    column = [[z * 8 + c for z in range(4)] for c in range(8)]
    rotations = cayley_blocks(skew_params, pairing)
    slab = lax.all_to_all(weight_slab, "tensor", split_axis=1, concat_axis=0, axis_index_groups=plane, tiled=True)
    local = token_rows.reshape(32, 4, 8, 256)
    spread = lax.all_to_all(local, "tensor", split_axis=2, concat_axis=0, axis_index_groups=plane, tiled=True)
    spread = spread.reshape(256, 1024)
    rot_z = lax.all_gather(rotations[4:], "tensor", axis_index_groups=column, axis=1, tiled=True)
    rot_xy = lax.all_gather(rotations[:4], "tensor", axis_index_groups=plane, axis=1, tiled=True)
    spread = rotate_cols(spread, rot_z[1], 3)
    spread = rotate_cols(spread, rot_z[0], 2)
    features = lax.all_to_all(spread, "tensor", split_axis=1, concat_axis=0, axis_index_groups=column, tiled=True)
    features = lax.all_gather(features, "tensor", axis_index_groups=plane, axis=0)
    for section, distance in enumerate((0, 2, 3, 4)):
        slab = rotate_rows(slab, rot_xy[section], distance)
    partial = jnp.einsum("ptf,pfn->tn", features, slab.reshape(8, 256, 1024), preferred_element_type=jnp.float32)
    partial = partial.astype(jnp.bfloat16)
    landed = lax.all_to_all(partial, "tensor", split_axis=0, concat_axis=0, tiled=True)
    landed = landed.reshape(4, 8, 32, 1024).astype(jnp.float32).sum(axis=0)
    return landed.transpose(1, 0, 2).reshape(32, 8192).astype(jnp.bfloat16)


def solution(mesh):
    in_specs = (
        P(("layer", "tensor"), None),
        P(("layer", "tensor"), None),
        P("layer", "tensor", None, None),
        P("layer", None),
    )
    out_specs = P(("layer", "tensor"), None)
    return jax.shard_map(shards, mesh=mesh, in_specs=in_specs, out_specs=out_specs, check_vma=False)
```

```python
import jax
import jax.numpy as jnp
import numpy as np
from jax import lax
from jax.experimental import pallas as pl
from jax.experimental.pallas import tpu as pltpu
from jax.sharding import PartitionSpec as P

HALF = 64
BLK = 128


def pair_table(distance, count):
    stride = 1 << distance
    rows = []
    for group in range(count // (2 * stride)):
        for offset in range(stride):
            low = group * 2 * stride + offset
            member = low if low >> 1 & 1 == 0 else low + stride
            rows.append((low, low + stride, (member >> 2) * 2 + (member & 1)))
    return rows


def split_dot(left, right):
    left_hi = left.astype(jnp.bfloat16)
    left_lo = (left - left_hi.astype(jnp.float32)).astype(jnp.bfloat16)
    right_hi = right.astype(jnp.bfloat16)
    right_lo = (right - right_hi.astype(jnp.float32)).astype(jnp.bfloat16)
    return jnp.dot(
        jnp.concatenate([left_hi, left_hi, left_lo], axis=1),
        jnp.concatenate([right_hi, right_lo, right_hi], axis=0),
        preferred_element_type=jnp.float32,
    )


def full_dot(left, right):
    return jnp.dot(left, right, precision=lax.Precision.HIGHEST, preferred_element_type=jnp.float32)


def rotation_kernel(skew_ref, pairing_ref, out_ref, gram, guess):
    count = gram.shape[0]
    rows = lax.broadcasted_iota(jnp.int32, (BLK, BLK), 0)
    lanes = lax.broadcasted_iota(jnp.int32, (BLK, BLK), 1)
    identity = (rows == lanes).astype(jnp.float32)
    largest = jnp.zeros((1, BLK), jnp.float32)
    for block in range(count):
        raw = skew_ref[block]
        skewed = raw - raw.T
        square = full_dot(skewed, skewed)
        gram[block] = identity - square
        largest = jnp.maximum(largest, jnp.sum(square * square, axis=0, keepdims=True).sum(axis=1, keepdims=True))
    top = 1.0 + jnp.sqrt(0.5 * jnp.max(largest)) * 1.0001
    start = 2.0 / (1.0 + top)
    for block in range(count):
        guess[block] = identity * start

    def more(state):
        return state > 5e-3

    def improve(spread):
        shrunk = spread * spread / (2.0 - spread * spread)
        scale = 2.0 / (2.0 - spread * spread)
        for block in range(count):
            now = guess[block]
            left = 2.0 * identity - split_dot(gram[block], now)
            guess[block] = scale * split_dot(now, left)
        return shrunk

    lax.while_loop(more, improve, (top - 1.0) / (top + 1.0))
    for block in range(count):
        raw = skew_ref[block]
        raised = identity + raw - raw.T
        now = guess[block]
        now = now + split_dot(now, identity - full_dot(gram[block], now))
        rotation = (2.0 * full_dot(now, raised) - identity).astype(jnp.bfloat16)
        order = pairing_ref[pl.ds(block // 2, 1), :]
        chosen = (rows == order).astype(jnp.bfloat16)
        inner = jnp.dot(chosen, rotation, preferred_element_type=jnp.float32).astype(jnp.bfloat16)
        outer = lax.dot_general(inner, chosen, (((1,), (1,)), ((), ())), preferred_element_type=jnp.float32)
        out_ref[block] = outer.astype(jnp.bfloat16)


def cayley_blocks(skew_params, pairing):
    sections, owned = skew_params.shape[:2]
    count = sections * owned
    out = pl.pallas_call(
        rotation_kernel,
        out_shape=jax.ShapeDtypeStruct((count, BLK, BLK), jnp.bfloat16),
        in_specs=[pl.BlockSpec(memory_space=pltpu.VMEM)] * 2,
        out_specs=pl.BlockSpec(memory_space=pltpu.VMEM),
        scratch_shapes=[pltpu.VMEM((count, BLK, BLK), jnp.float32)] * 2,
        cost_estimate=pl.CostEstimate(flops=count * BLK**3 * 20, bytes_accessed=count * BLK * BLK * 6, transcendentals=0),
    )(skew_params.reshape(count, BLK, BLK), pairing)
    return out.reshape(sections, owned, BLK, BLK)


def halves_dot(value, rotation_of, distance):
    halves = value.shape[1] // HALF
    parts = [None] * halves
    for low, high, owner in pair_table(distance, halves):
        joined = jnp.concatenate([value[:, low * HALF:(low + 1) * HALF], value[:, high * HALF:(high + 1) * HALF]], axis=1)
        turned = jnp.dot(joined, rotation_of(owner), preferred_element_type=jnp.float32).astype(jnp.bfloat16)
        parts[low], parts[high] = turned[:, :HALF], turned[:, HALF:]
    return jnp.concatenate(parts, axis=1)


def place():
    me = lax.axis_index("tensor")
    return me, me // 8, (me // 2) % 4, me % 2


def remote(src, dst, send, recv, peer):
    return pltpu.make_async_remote_copy(
        src_ref=src, dst_ref=dst, send_sem=send, recv_sem=recv,
        device_id={"tensor": peer}, device_id_type=pl.DeviceIdType.MESH,
    )


def greet(peers):
    barrier = pltpu.get_barrier_semaphore()
    for peer in peers:
        pl.semaphore_signal(barrier, inc=1, device_id={"tensor": peer}, device_id_type=pl.DeviceIdType.MESH)
    pl.semaphore_wait(barrier, len(peers))


def token_kernel(rows_ref, rot_ref, out_ref, rot_z, rot_x, rot_y, first, second, third, landed, send_e, recv_e, send_1, recv_1, send_2, recv_2):
    me, z, x, y = place()
    barrier = pltpu.get_barrier_semaphore()

    def signal(step, carry):
        pl.semaphore_signal(barrier, inc=1, device_id={"tensor": (me + step) % 32}, device_id_type=pl.DeviceIdType.MESH)
        return carry

    lax.fori_loop(1, 32, signal, 0)
    pl.semaphore_wait(barrier, 31)

    gathers = []
    for step in range(1, 4):
        gathers.append(remote(rot_ref.at[pl.ds(4, 2)], rot_z.at[:, z], send_e.at[step - 1], recv_e.at[step - 1], ((z + step) % 4) * 8 + x * 2 + y))
    for step in range(1, 4):
        gathers.append(remote(rot_ref.at[pl.ds(2, 2)], rot_x.at[:, x], send_e.at[2 + step], recv_e.at[2 + step], z * 8 + ((x + step) % 4) * 2 + y))
    gathers.append(remote(rot_ref.at[pl.ds(0, 2)], rot_y.at[:, y], send_e.at[6], recv_e.at[6], z * 8 + x * 2 + 1 - y))
    for gather in gathers:
        gather.start()
    rot_z[:, z] = rot_ref[4:6]
    rot_x[:, x] = rot_ref[2:4]
    rot_y[:, y] = rot_ref[0:2]

    for gather in gathers[:3]:
        gather.wait_recv()
    value = rows_ref[...]
    value = halves_dot(value, lambda k: rot_z[1, k // 2, k % 2], 3)
    value = halves_dot(value, lambda k: rot_z[0, k // 2, k % 2], 2)
    for piece in range(4):
        first[piece] = value[:, piece * 256:(piece + 1) * 256]
    moves = [remote(first.at[piece], second.at[x], send_1.at[piece], recv_1.at[x], piece * 8 + z * 2 + y) for piece in range(4)]
    for piece in range(4):
        @pl.when(jnp.logical_or(z != piece, x != z))
        def _():
            moves[piece].start()

    @pl.when(x == z)
    def _():
        second[x] = first[z]

    for piece in range(4):
        @pl.when(jnp.logical_or(z != x, x != piece))
        def _():
            remote(first.at[0], second.at[piece], send_1.at[0], recv_1.at[piece], me).wait_recv()
    for gather in gathers[3:6]:
        gather.wait_recv()
    value = jnp.concatenate([second[piece] for piece in range(4)], axis=1)
    value = halves_dot(value, lambda k: rot_x[1, k // 2, k % 2], 3)
    value = halves_dot(value, lambda k: rot_x[0, k // 2, k % 2], 2)
    for piece in range(4):
        third[piece] = value[:, piece * 256:(piece + 1) * 256]
    spreads = []
    for other in range(8):
        to_x, to_y = other // 2, other % 2
        spreads.append(remote(third.at[to_x], landed.at[x * 2 + y], send_2.at[other], recv_2.at[x * 2 + y], z * 8 + other))
    for other in range(8):
        @pl.when(other != x * 2 + y)
        def _():
            spreads[other].start()
    landed[x * 2 + y] = third[x]
    gathers[6].wait_recv()
    for group in range(4):
        for side in range(2):
            other = group * 2 + side

            @pl.when(other != x * 2 + y)
            def _():
                remote(third.at[0], landed.at[other], send_2.at[0], recv_2.at[other], me).wait_recv()
        value = jnp.concatenate([landed[group * 2], landed[group * 2 + 1]], axis=1)
        value = halves_dot(value, lambda k: rot_y[1, k // 2, k % 2], 2)
        value = halves_dot(value, lambda k: rot_y[0, k // 2, k % 2], 0)
        out_ref[group] = value
    for gather in gathers:
        gather.wait_send()
    for piece in range(4):
        @pl.when(jnp.logical_or(z != piece, x != z))
        def _():
            moves[piece].wait_send()
    for other in range(8):
        @pl.when(other != x * 2 + y)
        def _():
            spreads[other].wait_send()


def turn_tokens(rows, rotations):
    bf = jnp.bfloat16
    return pl.pallas_call(
        token_kernel,
        out_shape=jax.ShapeDtypeStruct((4, 256, 512), bf),
        in_specs=[pl.BlockSpec(memory_space=pltpu.VMEM)] * 2,
        out_specs=pl.BlockSpec(memory_space=pltpu.VMEM),
        scratch_shapes=[
            pltpu.VMEM((2, 4, 2, BLK, BLK), bf),
            pltpu.VMEM((2, 4, 2, BLK, BLK), bf),
            pltpu.VMEM((2, 2, 2, BLK, BLK), bf),
            pltpu.VMEM((4, 256, 256), bf),
            pltpu.VMEM((4, 256, 256), bf),
            pltpu.VMEM((4, 256, 256), bf),
            pltpu.VMEM((8, 256, 256), bf),
            pltpu.SemaphoreType.DMA((7,)),
            pltpu.SemaphoreType.DMA((7,)),
            pltpu.SemaphoreType.DMA((4,)),
            pltpu.SemaphoreType.DMA((4,)),
            pltpu.SemaphoreType.DMA((8,)),
            pltpu.SemaphoreType.DMA((8,)),
        ],
        compiler_params=pltpu.CompilerParams(collective_id=1, has_side_effects=True),
        cost_estimate=pl.CostEstimate(flops=20 * 10**9, bytes_accessed=40 * 2**20, transcendentals=0),
    )(rows, rotations)


def project_kernel(tok_ref, own_ref, other_ref, out_ref, slab, part, far, near, part2, far2, near2, last, swapped, send, recv, send_y, recv_y, load):
    me, z, x, y = place()
    coords = (z, x)

    def peer(axis, step):
        if axis == 0:
            return ((z + step) % 4) * 8 + x * 2 + y
        return z * 8 + ((x + step) % 4) * 2 + y

    partner = z * 8 + x * 2 + 1 - y
    loads = [
        pltpu.make_async_copy(own_ref.at[:, pl.ds(pl.multiple_of(y * 4096, 4096), 4096)], slab.at[pl.ds(pl.multiple_of(y * 256, 256), 256)], load.at[0]),
        pltpu.make_async_copy(other_ref, slab.at[pl.ds(pl.multiple_of((1 - y) * 256, 256), 256)], load.at[1]),
    ]
    for copy in loads:
        copy.start()
    greet([peer(0, 1), peer(0, 3), peer(1, 1), peer(1, 3), partner])
    for copy in loads:
        copy.wait()

    def compute(color, role):
        block = (coords[color] + role) % 4
        if color == 0:
            left = tok_ref[block]
        else:
            left = jnp.concatenate([tok_ref[group, pl.ds(pl.multiple_of(block * 64, 64), 64), :] for group in range(4)], axis=0)

        def tile(step, carry):
            at = pl.multiple_of(color * 2048 + step * 512, 512)
            part[color, role, step] = jnp.dot(left, slab[:, pl.ds(at, 512)], preferred_element_type=jnp.float32).astype(jnp.bfloat16)
            return carry

        lax.fori_loop(0, 4, tile, 0)

    pending = []

    def ship(stage, color, slot, src, dst, step):
        axis = color if stage == 0 else 1 - color
        copy = remote(src, dst, send.at[stage, color, slot], recv.at[stage, color, slot], peer(axis, step))
        copy.start()
        pending.append(copy)
        return copy

    def start_far(stage, color, source, far_buf):
        up = ship(stage, color, 0, source.at[color, 2, pl.ds(0, 2)], far_buf.at[color, 0], 1)
        down = ship(stage, color, 1, source.at[color, 2, pl.ds(2, 2)], far_buf.at[color, 1], 3)
        return up, down

    def start_plain(stage, color, source, near_buf):
        up = ship(stage, color, 2, source.at[color, 1, pl.ds(2, 2)], near_buf.at[color, 0, pl.ds(2, 2)], 1)
        down = ship(stage, color, 3, source.at[color, 3, pl.ds(0, 2)], near_buf.at[color, 1, pl.ds(0, 2)], 3)
        return up, down

    def add(a, b):
        return (a.astype(jnp.float32) + b.astype(jnp.float32)).astype(jnp.bfloat16)

    def relay(stage, color, source, far_buf, near_buf, fars):
        fars[0].wait_recv()
        for tile in range(2):
            source[color, 1, tile] = add(source[color, 1, tile], far_buf[color, 0, tile])
        up = ship(stage, color, 4, source.at[color, 1, pl.ds(0, 2)], near_buf.at[color, 0, pl.ds(0, 2)], 1)
        fars[1].wait_recv()
        for tile in range(2):
            source[color, 3, 2 + tile] = add(source[color, 3, 2 + tile], far_buf[color, 1, tile])
        down = ship(stage, color, 5, source.at[color, 3, pl.ds(2, 2)], near_buf.at[color, 1, pl.ds(2, 2)], 3)
        return up, down

    fars, plains, relays = {}, {}, {}
    for color in range(2):
        compute(color, 2)
        fars[color] = start_far(0, color, part, far)
    for color in range(2):
        for role in (1, 3):
            compute(color, role)
        plains[color] = start_plain(0, color, part, near)
    for color in range(2):
        compute(color, 0)
    for color in range(2):
        relays[color] = relay(0, color, part, far, near, fars[color])

    fars2, plains2, relays2 = {}, {}, {}
    for color in range(2):
        for copy in plains[color] + relays[color]:
            copy.wait_recv()
        here = coords[1 - color]
        for role in (2, 1, 3, 0):
            at = pl.ds(pl.multiple_of((here + role) % 4 * 64, 64), 64)
            for tile in range(4):
                total = part[color, 0, tile, at, :].astype(jnp.float32)
                total = total + near[color, 0, tile, at, :].astype(jnp.float32) + near[color, 1, tile, at, :].astype(jnp.float32)
                part2[color, role, tile] = total.astype(jnp.bfloat16)
        fars2[color] = start_far(1, color, part2, far2)
        plains2[color] = start_plain(1, color, part2, near2)
    for color in range(2):
        relays2[color] = relay(1, color, part2, far2, near2, fars2[color])
    for color in range(2):
        for copy in plains2[color] + relays2[color]:
            copy.wait_recv()
        for tile in range(4):
            total = part2[color, 0, tile].astype(jnp.float32)
            total = total + near2[color, 0, tile].astype(jnp.float32) + near2[color, 1, tile].astype(jnp.float32)
            at = color * 2048 + tile * 512
            total = total.astype(jnp.bfloat16)
            last[0, :, at:at + 512] = total[:32]
            last[1, :, at:at + 512] = total[32:]
    swap = remote(last.at[1 - y], swapped, send_y, recv_y, partner)
    swap.start()
    out_ref[:, pl.ds(pl.multiple_of(y * 4096, 4096), 4096)] = last[y]
    swap.wait_recv()
    out_ref[:, pl.ds(pl.multiple_of((1 - y) * 4096, 4096), 4096)] = swapped[...]
    swap.wait_send()
    for copy in pending:
        copy.wait_send()


def project(tokens, slab, received):
    bf = jnp.bfloat16
    return pl.pallas_call(
        project_kernel,
        out_shape=jax.ShapeDtypeStruct((32, 8192), bf),
        in_specs=[
            pl.BlockSpec(memory_space=pltpu.VMEM),
            pl.BlockSpec(memory_space=pl.ANY),
            pl.BlockSpec(memory_space=pl.ANY),
        ],
        out_specs=pl.BlockSpec(memory_space=pltpu.VMEM),
        scratch_shapes=[
            pltpu.VMEM((512, 4096), bf),
            pltpu.VMEM((2, 4, 4, 256, 512), bf),
            pltpu.VMEM((2, 2, 2, 256, 512), bf),
            pltpu.VMEM((2, 2, 4, 256, 512), bf),
            pltpu.VMEM((2, 4, 4, 64, 512), bf),
            pltpu.VMEM((2, 2, 2, 64, 512), bf),
            pltpu.VMEM((2, 2, 4, 64, 512), bf),
            pltpu.VMEM((2, 32, 4096), bf),
            pltpu.VMEM((32, 4096), bf),
            pltpu.SemaphoreType.DMA((2, 2, 6)),
            pltpu.SemaphoreType.DMA((2, 2, 6)),
            pltpu.SemaphoreType.DMA,
            pltpu.SemaphoreType.DMA,
            pltpu.SemaphoreType.DMA((2,)),
        ],
        compiler_params=pltpu.CompilerParams(collective_id=2, has_side_effects=True, vmem_limit_bytes=48 * 2**20),
        cost_estimate=pl.CostEstimate(flops=2 * 1024 * 512 * 4096, bytes_accessed=10 * 2**20, transcendentals=0),
    )(tokens, slab, received)


def shards(weight_slab, token_rows, skew_params, pairing):
    side = lax.axis_index("tensor") % 2
    plane = [[z * 8 + c for c in range(8)] for z in range(4)]
    outgoing = lax.dynamic_slice_in_dim(weight_slab, (1 - side) * 4096, 4096, 1)
    received = lax.ppermute(outgoing, "tensor", [(d, d ^ 1) for d in range(32)])
    local = token_rows.reshape(32, 4, 8, 256)
    spread = lax.all_to_all(local, "tensor", split_axis=2, concat_axis=0, axis_index_groups=plane, tiled=True)
    rotations = cayley_blocks(skew_params, pairing)
    tokens = turn_tokens(spread.reshape(256, 1024), rotations)
    return project(tokens, weight_slab, received)


def solution(mesh):
    in_specs = (
        P(("layer", "tensor"), None),
        P(("layer", "tensor"), None),
        P("layer", "tensor", None, None),
        P("layer", None),
    )
    out_specs = P(("layer", "tensor"), None)
    return jax.shard_map(shards, mesh=mesh, in_specs=in_specs, out_specs=out_specs, check_vma=False)
```

```python
import jax
import jax.numpy as jnp
import numpy as np
from jax import lax
from jax.experimental import pallas as pl
from jax.experimental.pallas import tpu as pltpu
from jax.sharding import PartitionSpec as P

HALF = 64
BLK = 128


def pair_table(distance, count):
    stride = 1 << distance
    rows = []
    for group in range(count // (2 * stride)):
        for offset in range(stride):
            low = group * 2 * stride + offset
            member = low if low >> 1 & 1 == 0 else low + stride
            rows.append((low, low + stride, (member >> 2) * 2 + (member & 1)))
    return rows


def split_dot(left, right):
    left_hi = left.astype(jnp.bfloat16)
    left_lo = (left - left_hi.astype(jnp.float32)).astype(jnp.bfloat16)
    right_hi = right.astype(jnp.bfloat16)
    right_lo = (right - right_hi.astype(jnp.float32)).astype(jnp.bfloat16)
    return jnp.dot(
        jnp.concatenate([left_hi, left_hi, left_lo], axis=1),
        jnp.concatenate([right_hi, right_lo, right_hi], axis=0),
        preferred_element_type=jnp.float32,
    )


def full_dot(left, right):
    return jnp.dot(left, right, precision=lax.Precision.HIGHEST, preferred_element_type=jnp.float32)


def rotation_kernel(skew_ref, pairing_ref, out_ref, gram, guess):
    count = gram.shape[0]
    rows = lax.broadcasted_iota(jnp.int32, (BLK, BLK), 0)
    lanes = lax.broadcasted_iota(jnp.int32, (BLK, BLK), 1)
    identity = (rows == lanes).astype(jnp.float32)
    largest = jnp.zeros((1, 1), jnp.float32)
    for block in range(count):
        raw = skew_ref[block]
        skewed = raw - raw.T
        square = full_dot(skewed, skewed)
        gram[block] = identity - square
        rounded = square.astype(jnp.bfloat16)
        fourth = jnp.dot(rounded, rounded, preferred_element_type=jnp.float32)
        largest = jnp.maximum(largest, jnp.sum(jnp.sum(fourth * fourth, axis=0, keepdims=True), axis=1, keepdims=True))
    top = 1.0 + 1.02 * jnp.sqrt(jnp.sqrt(0.5 * jnp.max(largest)))
    start = 2.0 / (1.0 + top)
    for block in range(count):
        guess[block] = identity * start

    def more(state):
        return state > 1e-2

    def improve(spread):
        shrunk = spread * spread / (2.0 - spread * spread)
        scale = 2.0 / (2.0 - spread * spread)
        for block in range(count):
            now = guess[block]
            left = 2.0 * identity - split_dot(gram[block], now)
            guess[block] = scale * split_dot(now, left)
        return shrunk

    lax.while_loop(more, improve, (top - 1.0) / (top + 1.0))
    for block in range(count):
        raw = skew_ref[block]
        raised = identity + raw - raw.T
        now = guess[block]
        now = now + split_dot(now, identity - full_dot(gram[block], now))
        rotation = (2.0 * split_dot(now, raised) - identity).astype(jnp.bfloat16)
        order = pairing_ref[pl.ds(block // 2, 1), :]
        chosen = (rows == order).astype(jnp.bfloat16)
        inner = jnp.dot(chosen, rotation, preferred_element_type=jnp.float32).astype(jnp.bfloat16)
        outer = lax.dot_general(inner, chosen, (((1,), (1,)), ((), ())), preferred_element_type=jnp.float32)
        out_ref[block] = outer.astype(jnp.bfloat16)


def cayley_blocks(skew_params, pairing):
    sections, owned = skew_params.shape[:2]
    count = sections * owned
    out = pl.pallas_call(
        rotation_kernel,
        out_shape=jax.ShapeDtypeStruct((count, BLK, BLK), jnp.bfloat16),
        in_specs=[pl.BlockSpec(memory_space=pltpu.VMEM)] * 2,
        out_specs=pl.BlockSpec(memory_space=pltpu.VMEM),
        scratch_shapes=[pltpu.VMEM((count, BLK, BLK), jnp.float32)] * 2,
        cost_estimate=pl.CostEstimate(flops=count * BLK**3 * 20, bytes_accessed=count * BLK * BLK * 6, transcendentals=0),
    )(skew_params.reshape(count, BLK, BLK), pairing)
    return out.reshape(sections, owned, BLK, BLK)


def halves_dot(value, rotation_of, distance):
    halves = value.shape[1] // HALF
    parts = [None] * halves
    for low, high, owner in pair_table(distance, halves):
        joined = jnp.concatenate([value[:, low * HALF:(low + 1) * HALF], value[:, high * HALF:(high + 1) * HALF]], axis=1)
        turned = jnp.dot(joined, rotation_of(owner), preferred_element_type=jnp.float32).astype(jnp.bfloat16)
        parts[low], parts[high] = turned[:, :HALF], turned[:, HALF:]
    return jnp.concatenate(parts, axis=1)


def place():
    me = lax.axis_index("tensor")
    return me, me // 8, (me // 2) % 4, me % 2


def remote(src, dst, send, recv, peer):
    return pltpu.make_async_remote_copy(
        src_ref=src, dst_ref=dst, send_sem=send, recv_sem=recv,
        device_id={"tensor": peer}, device_id_type=pl.DeviceIdType.MESH,
    )


def greet(peers):
    barrier = pltpu.get_barrier_semaphore()
    for peer in peers:
        pl.semaphore_signal(barrier, inc=1, device_id={"tensor": peer}, device_id_type=pl.DeviceIdType.MESH)
    pl.semaphore_wait(barrier, len(peers))


def token_kernel(rows_ref, rot_ref, out_ref, rot_z, rot_x, rot_y, start, first, mid, second, third, landed, send_0, recv_0, send_e, recv_e, send_1, recv_1, send_2, recv_2, send_3, recv_3, send_4, recv_4):
    me, z, x, y = place()
    spot = x * 2 + y
    barrier = pltpu.get_barrier_semaphore()

    def signal(step, carry):
        pl.semaphore_signal(barrier, inc=1, device_id={"tensor": (me + step) % 32}, device_id_type=pl.DeviceIdType.MESH)
        return carry

    lax.fori_loop(1, 32, signal, 0)
    pl.semaphore_wait(barrier, 31)

    def gather(slot, source, target, peer):
        return remote(source, target, send_e.at[slot], recv_e.at[slot], peer)

    gathers_z = [gather(step - 1, rot_ref.at[pl.ds(4, 2)], rot_z.at[:, z], ((z + step) % 4) * 8 + spot) for step in (1, 3, 2)]
    gathers_x = [gather(2 + step, rot_ref.at[pl.ds(2, 2)], rot_x.at[:, x], z * 8 + ((x + step) % 4) * 2 + y) for step in (1, 3, 2)]
    gather_y = gather(6, rot_ref.at[pl.ds(0, 2)], rot_y.at[:, y], z * 8 + x * 2 + 1 - y)
    for copy in gathers_z:
        copy.start()

    def piece_of(other, group):
        at = pl.multiple_of(group * 2048 + other * 256, 256)
        return rows_ref.at[:, pl.ds(at, 256)]

    for step in range(1, 8):
        other = (spot + step) % 8
        for group in range(4):
            remote(piece_of(other, group), start.at[spot, :, pl.ds(group * 256, 256)], send_0.at[step], recv_0.at[spot], z * 8 + other).start()
    for group in range(4):
        start[spot, :, group * 256:(group + 1) * 256] = rows_ref[:, pl.ds(pl.multiple_of(group * 2048 + spot * 256, 256), 256)]
    rot_z[:, z] = rot_ref[4:6]
    rot_x[:, x] = rot_ref[2:4]
    rot_y[:, y] = rot_ref[0:2]
    for step in range(1, 8):
        other = (spot + step) % 8
        remote(start.at[spot], start.at[other], send_0.at[step], recv_0.at[other], me).wait_recv()
    for copy in gathers_z:
        copy.wait_recv()
    for copy in gathers_x:
        copy.start()
    gather_y.start()
    value = jnp.concatenate([start[other] for other in range(8)], axis=0)
    value = halves_dot(value, lambda k: rot_z[1, k // 2, k % 2], 3)
    value = halves_dot(value, lambda k: rot_z[0, k // 2, k % 2], 2)
    for piece in range(4):
        first[piece] = value[:, piece * 256:(piece + 1) * 256]

    over_z = [remote(first.at[(z + step) % 4], mid.at[z], send_1.at[step], recv_1.at[z], ((z + step) % 4) * 8 + spot) for step in (1, 3, 2)]
    for copy in over_z:
        copy.start()
    mid[z] = first[z]

    def onward(group):
        return remote(mid.at[group], second.at[x], send_2.at[group], recv_2.at[x], z * 8 + group * 2 + y)

    for step in (0, 3, 1, 2):
        group = (z + step) % 4
        if step != 0:
            remote(first.at[0], mid.at[group], send_1.at[step], recv_1.at[group], me).wait_recv()

        @pl.when(group != x)
        def _():
            onward(group).start()

        @pl.when(group == x)
        def _():
            second[x] = mid[group]

    for step in (1, 3, 2):
        source = (x + step) % 4
        remote(mid.at[0], second.at[source], send_2.at[0], recv_2.at[source], me).wait_recv()
    for copy in gathers_x:
        copy.wait_recv()
    value = jnp.concatenate([second[piece] for piece in range(4)], axis=1)
    value = halves_dot(value, lambda k: rot_x[1, k // 2, k % 2], 3)
    value = halves_dot(value, lambda k: rot_x[0, k // 2, k % 2], 2)
    for piece in range(4):
        third[piece] = value[:, piece * 256:(piece + 1) * 256]

    over_x = [remote(third.at[(x + step) % 4], landed.at[y, x], send_3.at[step], recv_3.at[x], z * 8 + ((x + step) % 4) * 2 + y) for step in (1, 3, 2)]
    for copy in over_x:
        copy.start()
    landed[y, x] = third[x]

    def across(group):
        return remote(landed.at[y, group], landed.at[y, group], send_4.at[group], recv_4.at[group], z * 8 + x * 2 + 1 - y)

    for step in (0, 3, 1, 2):
        group = (x + step) % 4
        if step != 0:
            remote(third.at[0], landed.at[y, group], send_3.at[step], recv_3.at[group], me).wait_recv()
        across(group).start()
    gather_y.wait_recv()
    for step in (0, 3, 1, 2):
        group = (x + step) % 4
        remote(landed.at[y, group], landed.at[1 - y, group], send_4.at[group], recv_4.at[group], me).wait_recv()
        value = jnp.concatenate([landed[0, group], landed[1, group]], axis=1)
        value = halves_dot(value, lambda k: rot_y[1, k // 2, k % 2], 2)
        value = halves_dot(value, lambda k: rot_y[0, k // 2, k % 2], 0)
        out_ref[group] = value
    for copy in gathers_z + gathers_x + [gather_y] + over_z + over_x:
        copy.wait_send()
    for step in range(1, 8):
        remote(start.at[spot], start.at[spot], send_0.at[step], recv_0.at[spot], me).wait_send()
    for group in range(4):
        across(group).wait_send()

        @pl.when(group != x)
        def _():
            onward(group).wait_send()


def turn_tokens(rows, rotations):
    bf = jnp.bfloat16
    return pl.pallas_call(
        token_kernel,
        out_shape=jax.ShapeDtypeStruct((4, 256, 512), bf),
        in_specs=[pl.BlockSpec(memory_space=pltpu.VMEM)] * 2,
        out_specs=pl.BlockSpec(memory_space=pltpu.VMEM),
        scratch_shapes=[
            pltpu.VMEM((2, 4, 2, BLK, BLK), bf),
            pltpu.VMEM((2, 4, 2, BLK, BLK), bf),
            pltpu.VMEM((2, 2, 2, BLK, BLK), bf),
            pltpu.VMEM((8, 32, 1024), bf),
            pltpu.VMEM((4, 256, 256), bf),
            pltpu.VMEM((4, 256, 256), bf),
            pltpu.VMEM((4, 256, 256), bf),
            pltpu.VMEM((4, 256, 256), bf),
            pltpu.VMEM((2, 4, 256, 256), bf),
        ] + [pltpu.SemaphoreType.DMA((count,)) for count in (8, 8, 7, 7, 4, 4, 4, 4, 4, 4, 4, 4)],
        compiler_params=pltpu.CompilerParams(collective_id=1, has_side_effects=True),
        cost_estimate=pl.CostEstimate(flops=20 * 10**9, bytes_accessed=40 * 2**20, transcendentals=0),
    )(rows, rotations)


def half_kernel(slab_ref, out_ref, done):
    side = lax.axis_index("tensor") % 2
    at = pl.multiple_of((1 - side) * 4096, 4096)
    copy = pltpu.make_async_copy(slab_ref.at[:, pl.ds(at, 4096)], out_ref, done)
    copy.start()
    copy.wait()


def partner_half(slab):
    return pl.pallas_call(
        half_kernel,
        out_shape=jax.ShapeDtypeStruct((256, 4096), jnp.bfloat16),
        in_specs=[pl.BlockSpec(memory_space=pl.ANY)],
        out_specs=pl.BlockSpec(memory_space=pltpu.VMEM),
        scratch_shapes=[pltpu.SemaphoreType.DMA],
        cost_estimate=pl.CostEstimate(flops=0, bytes_accessed=4 * 2**20, transcendentals=0),
    )(slab)


def project_kernel(tok_ref, own_ref, other_ref, out_ref, slab, part, far, near, part2, far2, near2, last, swapped, send, recv, send_y, recv_y, load):
    me, z, x, y = place()
    coords = (z, x)

    def peer(axis, step):
        if axis == 0:
            return ((z + step) % 4) * 8 + x * 2 + y
        return z * 8 + ((x + step) % 4) * 2 + y

    partner = z * 8 + x * 2 + 1 - y
    loads = [
        pltpu.make_async_copy(own_ref.at[:, pl.ds(pl.multiple_of(y * 4096, 4096), 4096)], slab.at[pl.ds(pl.multiple_of(y * 256, 256), 256)], load.at[0]),
        pltpu.make_async_copy(other_ref, slab.at[pl.ds(pl.multiple_of((1 - y) * 256, 256), 256)], load.at[1]),
    ]
    for copy in loads:
        copy.start()
    greet([peer(0, 1), peer(0, 3), peer(1, 1), peer(1, 3), partner])
    for copy in loads:
        copy.wait()

    def compute(color, role):
        block = (coords[color] + role) % 4
        if color == 0:
            left = tok_ref[block]
        else:
            left = jnp.concatenate([tok_ref[group, pl.ds(pl.multiple_of(block * 64, 64), 64), :] for group in range(4)], axis=0)

        def tile(step, carry):
            at = pl.multiple_of(color * 2048 + step * 512, 512)
            part[color, role, step] = jnp.dot(left, slab[:, pl.ds(at, 512)], preferred_element_type=jnp.float32).astype(jnp.bfloat16)
            return carry

        lax.fori_loop(0, 4, tile, 0)

    pending = []

    def ship(stage, color, slot, src, dst, step):
        axis = color if stage == 0 else 1 - color
        copy = remote(src, dst, send.at[stage, color, slot], recv.at[stage, color, slot], peer(axis, step))
        copy.start()
        pending.append(copy)
        return copy

    def start_far(stage, color, source, far_buf):
        up = ship(stage, color, 0, source.at[color, 2, pl.ds(0, 2)], far_buf.at[color, 0], 1)
        down = ship(stage, color, 1, source.at[color, 2, pl.ds(2, 2)], far_buf.at[color, 1], 3)
        return up, down

    def start_plain(stage, color, source, near_buf):
        up = ship(stage, color, 2, source.at[color, 1, pl.ds(2, 2)], near_buf.at[color, 0, pl.ds(2, 2)], 1)
        down = ship(stage, color, 3, source.at[color, 3, pl.ds(0, 2)], near_buf.at[color, 1, pl.ds(0, 2)], 3)
        return up, down

    def add(a, b):
        return (a.astype(jnp.float32) + b.astype(jnp.float32)).astype(jnp.bfloat16)

    def relay(stage, color, source, far_buf, near_buf, fars):
        fars[0].wait_recv()
        for tile in range(2):
            source[color, 1, tile] = add(source[color, 1, tile], far_buf[color, 0, tile])
        up = ship(stage, color, 4, source.at[color, 1, pl.ds(0, 2)], near_buf.at[color, 0, pl.ds(0, 2)], 1)
        fars[1].wait_recv()
        for tile in range(2):
            source[color, 3, 2 + tile] = add(source[color, 3, 2 + tile], far_buf[color, 1, tile])
        down = ship(stage, color, 5, source.at[color, 3, pl.ds(2, 2)], near_buf.at[color, 1, pl.ds(2, 2)], 3)
        return up, down

    fars, plains, relays = {}, {}, {}
    for color in range(2):
        compute(color, 2)
        fars[color] = start_far(0, color, part, far)
    for color in range(2):
        for role in (1, 3):
            compute(color, role)
        plains[color] = start_plain(0, color, part, near)
    for color in range(2):
        compute(color, 0)
    for color in range(2):
        relays[color] = relay(0, color, part, far, near, fars[color])

    fars2, plains2, relays2 = {}, {}, {}
    for color in range(2):
        for copy in plains[color] + relays[color]:
            copy.wait_recv()
        here = coords[1 - color]
        for role in (2, 1, 3, 0):
            at = pl.ds(pl.multiple_of((here + role) % 4 * 64, 64), 64)
            for tile in range(4):
                total = part[color, 0, tile, at, :].astype(jnp.float32)
                total = total + near[color, 0, tile, at, :].astype(jnp.float32) + near[color, 1, tile, at, :].astype(jnp.float32)
                part2[color, role, tile] = total.astype(jnp.bfloat16)
        fars2[color] = start_far(1, color, part2, far2)
        plains2[color] = start_plain(1, color, part2, near2)
    for color in range(2):
        relays2[color] = relay(1, color, part2, far2, near2, fars2[color])
    for color in range(2):
        for copy in plains2[color] + relays2[color]:
            copy.wait_recv()
        for tile in range(4):
            total = part2[color, 0, tile].astype(jnp.float32)
            total = total + near2[color, 0, tile].astype(jnp.float32) + near2[color, 1, tile].astype(jnp.float32)
            at = color * 2048 + tile * 512
            total = total.astype(jnp.bfloat16)
            last[0, :, at:at + 512] = total[:32]
            last[1, :, at:at + 512] = total[32:]
    swap = remote(last.at[1 - y], swapped, send_y, recv_y, partner)
    swap.start()
    out_ref[:, pl.ds(pl.multiple_of(y * 4096, 4096), 4096)] = last[y]
    swap.wait_recv()
    out_ref[:, pl.ds(pl.multiple_of((1 - y) * 4096, 4096), 4096)] = swapped[...]
    swap.wait_send()
    for copy in pending:
        copy.wait_send()


def project(tokens, slab, received):
    bf = jnp.bfloat16
    return pl.pallas_call(
        project_kernel,
        out_shape=jax.ShapeDtypeStruct((32, 8192), bf),
        in_specs=[
            pl.BlockSpec(memory_space=pltpu.VMEM),
            pl.BlockSpec(memory_space=pl.ANY),
            pl.BlockSpec(memory_space=pl.ANY),
        ],
        out_specs=pl.BlockSpec(memory_space=pltpu.VMEM),
        scratch_shapes=[
            pltpu.VMEM((512, 4096), bf),
            pltpu.VMEM((2, 4, 4, 256, 512), bf),
            pltpu.VMEM((2, 2, 2, 256, 512), bf),
            pltpu.VMEM((2, 2, 4, 256, 512), bf),
            pltpu.VMEM((2, 4, 4, 64, 512), bf),
            pltpu.VMEM((2, 2, 2, 64, 512), bf),
            pltpu.VMEM((2, 2, 4, 64, 512), bf),
            pltpu.VMEM((2, 32, 4096), bf),
            pltpu.VMEM((32, 4096), bf),
            pltpu.SemaphoreType.DMA((2, 2, 6)),
            pltpu.SemaphoreType.DMA((2, 2, 6)),
            pltpu.SemaphoreType.DMA,
            pltpu.SemaphoreType.DMA,
            pltpu.SemaphoreType.DMA((2,)),
        ],
        compiler_params=pltpu.CompilerParams(collective_id=2, has_side_effects=True, vmem_limit_bytes=48 * 2**20),
        cost_estimate=pl.CostEstimate(flops=2 * 1024 * 512 * 4096, bytes_accessed=10 * 2**20, transcendentals=0),
    )(tokens, slab, received)


def shards(weight_slab, token_rows, skew_params, pairing):
    received = lax.ppermute(partner_half(weight_slab), "tensor", [(d, d ^ 1) for d in range(32)])
    rotations = cayley_blocks(skew_params, pairing)
    tokens = turn_tokens(token_rows, rotations)
    return project(tokens, weight_slab, received)


def solution(mesh):
    in_specs = (
        P(("layer", "tensor"), None),
        P(("layer", "tensor"), None),
        P("layer", "tensor", None, None),
        P("layer", None),
    )
    out_specs = P(("layer", "tensor"), None)
    return jax.shard_map(shards, mesh=mesh, in_specs=in_specs, out_specs=out_specs, check_vma=False)
```

```python
import jax
import jax.numpy as jnp
import numpy as np
from jax import lax
from jax.experimental import pallas as pl
from jax.experimental.pallas import tpu as pltpu
from jax.sharding import PartitionSpec as P

HALF = 64
BLK = 128


def pair_table(distance, count):
    stride = 1 << distance
    rows = []
    for group in range(count // (2 * stride)):
        for offset in range(stride):
            low = group * 2 * stride + offset
            member = low if low >> 1 & 1 == 0 else low + stride
            rows.append((low, low + stride, (member >> 2) * 2 + (member & 1)))
    return rows


def split(value):
    high = value.astype(jnp.bfloat16)
    return high, (value - high.astype(jnp.float32)).astype(jnp.bfloat16)


def as_left(high, low):
    return jnp.concatenate([high, high, low], axis=1)


def as_right(high, low):
    return jnp.concatenate([high, low, high], axis=0)


def wide_dot(left, right):
    return jnp.dot(left, right, preferred_element_type=jnp.float32)


def full_dot(left, right):
    return jnp.dot(left, right, precision=lax.Precision.HIGHEST, preferred_element_type=jnp.float32)


def rotation_kernel(skew_ref, pairing_ref, out_ref, gram, gram_left, guess):
    count = gram.shape[0]
    rows = lax.broadcasted_iota(jnp.int32, (BLK, BLK), 0)
    lanes = lax.broadcasted_iota(jnp.int32, (BLK, BLK), 1)
    identity = (rows == lanes).astype(jnp.float32)
    largest = jnp.zeros((1, 1), jnp.float32)
    for block in range(count):
        raw = skew_ref[block]
        skewed = raw - raw.T
        square = full_dot(skewed, skewed)
        shifted = identity - square
        gram[block] = shifted
        gram_left[block] = as_left(*split(shifted))
        rounded = square.astype(jnp.bfloat16)
        fourth = jnp.dot(rounded, rounded, preferred_element_type=jnp.float32)
        largest = jnp.maximum(largest, jnp.sum(jnp.sum(fourth * fourth, axis=0, keepdims=True), axis=1, keepdims=True))
    top = 1.0 + 1.02 * jnp.sqrt(jnp.sqrt(0.5 * jnp.max(largest)))
    start = 2.0 / (1.0 + top)
    for block in range(count):
        guess[block] = identity * start

    def more(state):
        return state > 1e-2

    def improve(spread):
        shrunk = spread * spread / (2.0 - spread * spread)
        scale = 2.0 / (2.0 - spread * spread)
        for block in range(count):
            high, low = split(guess[block])
            left = 2.0 * identity - wide_dot(gram_left[block], as_right(high, low))
            guess[block] = scale * wide_dot(as_left(high, low), as_right(*split(left)))
        return shrunk

    lax.while_loop(more, improve, (top - 1.0) / (top + 1.0))
    for section in range(count // 2):
        turned = []
        for block in (2 * section, 2 * section + 1):
            raw = skew_ref[block]
            raised = identity + raw - raw.T
            now = guess[block]
            miss = identity - full_dot(gram[block], now)
            now = now + wide_dot(as_left(*split(now)), as_right(*split(miss)))
            rotation = 2.0 * wide_dot(as_left(*split(now)), as_right(*split(raised))) - identity
            turned.append(rotation.astype(jnp.bfloat16))
        order = pairing_ref[pl.ds(section, 1), :]
        chosen = (rows == order).astype(jnp.float32)
        inner = wide_dot(chosen.astype(jnp.bfloat16), jnp.concatenate(turned, axis=1)).astype(jnp.bfloat16)
        stacked = jnp.concatenate([inner[:, :BLK], inner[:, BLK:]], axis=0)
        outer = wide_dot(stacked, chosen.T.astype(jnp.bfloat16)).astype(jnp.bfloat16)
        out_ref[2 * section] = outer[:BLK]
        out_ref[2 * section + 1] = outer[BLK:]


def cayley_blocks(skew_params, pairing):
    sections, owned = skew_params.shape[:2]
    count = sections * owned
    out = pl.pallas_call(
        rotation_kernel,
        out_shape=jax.ShapeDtypeStruct((count, BLK, BLK), jnp.bfloat16),
        in_specs=[pl.BlockSpec(memory_space=pltpu.VMEM)] * 2,
        out_specs=pl.BlockSpec(memory_space=pltpu.VMEM),
        scratch_shapes=[
            pltpu.VMEM((count, BLK, BLK), jnp.float32),
            pltpu.VMEM((count, BLK, 3 * BLK), jnp.bfloat16),
            pltpu.VMEM((count, BLK, BLK), jnp.float32),
        ],
        cost_estimate=pl.CostEstimate(flops=count * BLK**3 * 20, bytes_accessed=count * BLK * BLK * 6, transcendentals=0),
    )(skew_params.reshape(count, BLK, BLK), pairing)
    return out.reshape(sections, owned, BLK, BLK)


def halves_dot(value, rotation_of, distance):
    halves = value.shape[1] // HALF
    parts = [None] * halves
    for low, high, owner in pair_table(distance, halves):
        joined = jnp.concatenate([value[:, low * HALF:(low + 1) * HALF], value[:, high * HALF:(high + 1) * HALF]], axis=1)
        turned = jnp.dot(joined, rotation_of(owner), preferred_element_type=jnp.float32).astype(jnp.bfloat16)
        parts[low], parts[high] = turned[:, :HALF], turned[:, HALF:]
    return jnp.concatenate(parts, axis=1)


def place():
    me = lax.axis_index("tensor")
    return me, me // 8, (me // 2) % 4, me % 2


def remote(src, dst, send, recv, peer):
    return pltpu.make_async_remote_copy(
        src_ref=src, dst_ref=dst, send_sem=send, recv_sem=recv,
        device_id={"tensor": peer}, device_id_type=pl.DeviceIdType.MESH,
    )


def greet(peers):
    barrier = pltpu.get_barrier_semaphore()
    for peer in peers:
        pl.semaphore_signal(barrier, inc=1, device_id={"tensor": peer}, device_id_type=pl.DeviceIdType.MESH)
    pl.semaphore_wait(barrier, len(peers))


def token_kernel(rows_ref, rot_ref, slab_ref, out_ref, late_ref, rot_z, rot_x, rot_y, start, first, mid, second, third, landed, send_0, recv_0, send_e, recv_e, send_1, recv_1, send_2, recv_2, send_3, recv_3, send_4, recv_4, send_w, recv_w):
    me, z, x, y = place()
    spot = x * 2 + y
    partner = z * 8 + x * 2 + 1 - y
    greet([((z + step) % 4) * 8 + spot for step in range(1, 4)] + [z * 8 + (spot + step) % 8 for step in range(1, 8)])

    def gather(slot, source, target, peer):
        return remote(source, target, send_e.at[slot], recv_e.at[slot], peer)

    gathers_z = [gather(step - 1, rot_ref.at[pl.ds(4, 2)], rot_z.at[:, z], ((z + step) % 4) * 8 + spot) for step in (1, 3, 2)]
    gathers_x = [gather(2 + step, rot_ref.at[pl.ds(2, 2)], rot_x.at[:, x], z * 8 + ((x + step) % 4) * 2 + y) for step in (1, 3, 2)]
    gather_y = gather(6, rot_ref.at[pl.ds(0, 2)], rot_y.at[:, y], z * 8 + x * 2 + 1 - y)
    for copy in gathers_z:
        copy.start()

    def piece_of(other, group):
        at = pl.multiple_of(group * 2048 + other * 256, 256)
        return rows_ref.at[:, pl.ds(at, 256)]

    for step in range(1, 8):
        other = (spot + step) % 8
        for group in range(4):
            remote(piece_of(other, group), start.at[spot, :, pl.ds(group * 256, 256)], send_0.at[step], recv_0.at[spot], z * 8 + other).start()
    gather_y.start()
    late = pl.multiple_of((1 - y) * 4096 + 2048, 2048)
    rest = remote(slab_ref.at[:, pl.ds(late, 2048)], late_ref, send_w, recv_w, partner)
    rest.start()
    for group in range(4):
        start[spot, :, group * 256:(group + 1) * 256] = rows_ref[:, pl.ds(pl.multiple_of(group * 2048 + spot * 256, 256), 256)]
    rot_z[:, z] = rot_ref[4:6]
    rot_x[:, x] = rot_ref[2:4]
    rot_y[:, y] = rot_ref[0:2]
    for step in range(1, 8):
        other = (spot + step) % 8
        remote(start.at[spot], start.at[other], send_0.at[step], recv_0.at[other], me).wait_recv()
    for copy in gathers_z:
        copy.wait_recv()
    for copy in gathers_x:
        copy.start()
    value = jnp.concatenate([start[other] for other in range(8)], axis=0)
    value = halves_dot(value, lambda k: rot_z[1, k // 2, k % 2], 3)
    value = halves_dot(value, lambda k: rot_z[0, k // 2, k % 2], 2)
    for piece in range(4):
        first[piece] = value[:, piece * 256:(piece + 1) * 256]

    over_z = [remote(first.at[(z + step) % 4], mid.at[z], send_1.at[step], recv_1.at[z], ((z + step) % 4) * 8 + spot) for step in (1, 3, 2)]
    for copy in over_z:
        copy.start()
    mid[z] = first[z]

    def onward(group):
        return remote(mid.at[group], second.at[x], send_2.at[group], recv_2.at[x], z * 8 + group * 2 + y)

    for step in (0, 3, 1, 2):
        group = (z + step) % 4
        if step != 0:
            remote(first.at[0], mid.at[group], send_1.at[step], recv_1.at[group], me).wait_recv()

        @pl.when(group != x)
        def _():
            onward(group).start()

        @pl.when(group == x)
        def _():
            second[x] = mid[group]

    for step in (1, 3, 2):
        source = (x + step) % 4
        remote(mid.at[0], second.at[source], send_2.at[0], recv_2.at[source], me).wait_recv()
    for copy in gathers_x:
        copy.wait_recv()
    value = jnp.concatenate([second[piece] for piece in range(4)], axis=1)
    value = halves_dot(value, lambda k: rot_x[1, k // 2, k % 2], 3)
    value = halves_dot(value, lambda k: rot_x[0, k // 2, k % 2], 2)
    for piece in range(4):
        third[piece] = value[:, piece * 256:(piece + 1) * 256]

    over_x = [remote(third.at[(x + step) % 4], landed.at[y, x], send_3.at[step], recv_3.at[x], z * 8 + ((x + step) % 4) * 2 + y) for step in (1, 3, 2)]
    for copy in over_x:
        copy.start()
    landed[y, x] = third[x]

    def across(group):
        return remote(landed.at[y, group], landed.at[y, group], send_4.at[group], recv_4.at[group], z * 8 + x * 2 + 1 - y)

    for step in (0, 3, 1, 2):
        group = (x + step) % 4
        if step != 0:
            remote(third.at[0], landed.at[y, group], send_3.at[step], recv_3.at[group], me).wait_recv()
        across(group).start()
    gather_y.wait_recv()
    for step in (0, 3, 1, 2):
        group = (x + step) % 4
        remote(landed.at[y, group], landed.at[1 - y, group], send_4.at[group], recv_4.at[group], me).wait_recv()
        value = jnp.concatenate([landed[0, group], landed[1, group]], axis=1)
        value = halves_dot(value, lambda k: rot_y[1, k // 2, k % 2], 2)
        value = halves_dot(value, lambda k: rot_y[0, k // 2, k % 2], 0)
        out_ref[group] = value
    rest.wait_recv()
    for copy in gathers_z + gathers_x + [gather_y, rest] + over_z + over_x:
        copy.wait_send()
    for step in range(1, 8):
        remote(start.at[spot], start.at[spot], send_0.at[step], recv_0.at[spot], me).wait_send()
    for group in range(4):
        across(group).wait_send()

        @pl.when(group != x)
        def _():
            onward(group).wait_send()


def turn_tokens(rows, rotations, slab):
    bf = jnp.bfloat16
    return pl.pallas_call(
        token_kernel,
        out_shape=(jax.ShapeDtypeStruct((4, 256, 512), bf), jax.ShapeDtypeStruct((256, 2048), bf)),
        in_specs=[pl.BlockSpec(memory_space=pltpu.VMEM)] * 2 + [pl.BlockSpec(memory_space=pl.ANY)],
        out_specs=(pl.BlockSpec(memory_space=pltpu.VMEM), pl.BlockSpec(memory_space=pl.ANY)),
        scratch_shapes=[
            pltpu.VMEM((2, 4, 2, BLK, BLK), bf),
            pltpu.VMEM((2, 4, 2, BLK, BLK), bf),
            pltpu.VMEM((2, 2, 2, BLK, BLK), bf),
            pltpu.VMEM((8, 32, 1024), bf),
            pltpu.VMEM((4, 256, 256), bf),
            pltpu.VMEM((4, 256, 256), bf),
            pltpu.VMEM((4, 256, 256), bf),
            pltpu.VMEM((4, 256, 256), bf),
            pltpu.VMEM((2, 4, 256, 256), bf),
        ] + [pltpu.SemaphoreType.DMA((count,)) for count in (8, 8, 7, 7, 4, 4, 4, 4, 4, 4, 4, 4)] + [pltpu.SemaphoreType.DMA] * 2,
        compiler_params=pltpu.CompilerParams(collective_id=1, has_side_effects=True),
        cost_estimate=pl.CostEstimate(flops=20 * 10**9, bytes_accessed=40 * 2**20, transcendentals=0),
    )(rows, rotations, slab)


def half_kernel(slab_ref, out_ref, done):
    side = lax.axis_index("tensor") % 2
    at = pl.multiple_of((1 - side) * 4096, 4096)
    copy = pltpu.make_async_copy(slab_ref.at[:, pl.ds(at, 2048)], out_ref, done)
    copy.start()
    copy.wait()


def partner_half(slab):
    return pl.pallas_call(
        half_kernel,
        out_shape=jax.ShapeDtypeStruct((256, 2048), jnp.bfloat16),
        in_specs=[pl.BlockSpec(memory_space=pl.ANY)],
        out_specs=pl.BlockSpec(memory_space=pltpu.VMEM),
        scratch_shapes=[pltpu.SemaphoreType.DMA],
        cost_estimate=pl.CostEstimate(flops=0, bytes_accessed=4 * 2**20, transcendentals=0),
    )(slab)


def project_kernel(tok_hbm, own_ref, early_ref, late_ref, out_ref, slab, part, far, near, part2, far2, near2, last, swapped, tok_ref, send, recv, send_y, recv_y, load):
    me, z, x, y = place()
    coords = (z, x)

    def peer(axis, step):
        if axis == 0:
            return ((z + step) % 4) * 8 + x * 2 + y
        return z * 8 + ((x + step) % 4) * 2 + y

    partner = z * 8 + x * 2 + 1 - y
    loads = [
        pltpu.make_async_copy(own_ref.at[:, pl.ds(pl.multiple_of(y * 4096, 4096), 4096)], slab.at[pl.ds(pl.multiple_of(y * 256, 256), 256)], load.at[0]),
        pltpu.make_async_copy(early_ref, slab.at[pl.ds(pl.multiple_of((1 - y) * 256, 256), 256), pl.ds(0, 2048)], load.at[1]),
        pltpu.make_async_copy(late_ref, slab.at[pl.ds(pl.multiple_of((1 - y) * 256, 256), 256), pl.ds(2048, 2048)], load.at[2]),
    ]
    loads.append(pltpu.make_async_copy(tok_hbm, tok_ref, load.at[3]))
    for copy in loads:
        copy.start()
    greet([peer(0, 1), peer(0, 3), peer(1, 1), peer(1, 3), partner])
    for copy in loads:
        copy.wait()

    def compute(color, role):
        block = (coords[color] + role) % 4
        if color == 0:
            left = tok_ref[block]
        else:
            left = jnp.concatenate([tok_ref[group, pl.ds(pl.multiple_of(block * 64, 64), 64), :] for group in range(4)], axis=0)

        def tile(step, carry):
            at = pl.multiple_of(color * 2048 + step * 512, 512)
            part[color, role, step] = jnp.dot(left, slab[:, pl.ds(at, 512)], preferred_element_type=jnp.float32).astype(jnp.bfloat16)
            return carry

        lax.fori_loop(0, 4, tile, 0)

    pending = []

    def ship(stage, color, slot, src, dst, step):
        axis = color if stage == 0 else 1 - color
        copy = remote(src, dst, send.at[stage, color, slot], recv.at[stage, color, slot], peer(axis, step))
        copy.start()
        pending.append(copy)
        return copy

    def start_far(stage, color, source, far_buf):
        up = ship(stage, color, 0, source.at[color, 2, pl.ds(0, 2)], far_buf.at[color, 0], 1)
        down = ship(stage, color, 1, source.at[color, 2, pl.ds(2, 2)], far_buf.at[color, 1], 3)
        return up, down

    def start_plain(stage, color, source, near_buf):
        up = ship(stage, color, 2, source.at[color, 1, pl.ds(2, 2)], near_buf.at[color, 0, pl.ds(2, 2)], 1)
        down = ship(stage, color, 3, source.at[color, 3, pl.ds(0, 2)], near_buf.at[color, 1, pl.ds(0, 2)], 3)
        return up, down

    def add(a, b):
        return (a.astype(jnp.float32) + b.astype(jnp.float32)).astype(jnp.bfloat16)

    def relay(stage, color, source, far_buf, near_buf, fars):
        fars[0].wait_recv()
        for tile in range(2):
            source[color, 1, tile] = add(source[color, 1, tile], far_buf[color, 0, tile])
        up = ship(stage, color, 4, source.at[color, 1, pl.ds(0, 2)], near_buf.at[color, 0, pl.ds(0, 2)], 1)
        fars[1].wait_recv()
        for tile in range(2):
            source[color, 3, 2 + tile] = add(source[color, 3, 2 + tile], far_buf[color, 1, tile])
        down = ship(stage, color, 5, source.at[color, 3, pl.ds(2, 2)], near_buf.at[color, 1, pl.ds(2, 2)], 3)
        return up, down

    fars, plains, relays = {}, {}, {}
    for color in range(2):
        compute(color, 2)
        fars[color] = start_far(0, color, part, far)
    for color in range(2):
        for role in (1, 3):
            compute(color, role)
        plains[color] = start_plain(0, color, part, near)
    for color in range(2):
        compute(color, 0)
    for color in range(2):
        relays[color] = relay(0, color, part, far, near, fars[color])

    fars2, plains2, relays2 = {}, {}, {}
    for color in range(2):
        for copy in plains[color] + relays[color]:
            copy.wait_recv()
        here = coords[1 - color]
        for role in (2, 1, 3, 0):
            at = pl.ds(pl.multiple_of((here + role) % 4 * 64, 64), 64)
            for tile in range(4):
                total = part[color, 0, tile, at, :].astype(jnp.float32)
                total = total + near[color, 0, tile, at, :].astype(jnp.float32) + near[color, 1, tile, at, :].astype(jnp.float32)
                part2[color, role, tile] = total.astype(jnp.bfloat16)
        fars2[color] = start_far(1, color, part2, far2)
        plains2[color] = start_plain(1, color, part2, near2)
    for color in range(2):
        relays2[color] = relay(1, color, part2, far2, near2, fars2[color])
    for color in range(2):
        for copy in plains2[color] + relays2[color]:
            copy.wait_recv()
        for tile in range(4):
            total = part2[color, 0, tile].astype(jnp.float32)
            total = total + near2[color, 0, tile].astype(jnp.float32) + near2[color, 1, tile].astype(jnp.float32)
            at = color * 2048 + tile * 512
            total = total.astype(jnp.bfloat16)
            last[0, :, at:at + 512] = total[:32]
            last[1, :, at:at + 512] = total[32:]
    swap = remote(last.at[1 - y], swapped, send_y, recv_y, partner)
    swap.start()
    out_ref[:, pl.ds(pl.multiple_of(y * 4096, 4096), 4096)] = last[y]
    swap.wait_recv()
    out_ref[:, pl.ds(pl.multiple_of((1 - y) * 4096, 4096), 4096)] = swapped[...]
    swap.wait_send()
    for copy in pending:
        copy.wait_send()


def project(tokens, slab, early, late):
    bf = jnp.bfloat16
    return pl.pallas_call(
        project_kernel,
        out_shape=jax.ShapeDtypeStruct((32, 8192), bf),
        in_specs=[
            pl.BlockSpec(memory_space=pltpu.HBM),
            pl.BlockSpec(memory_space=pltpu.HBM),
            pl.BlockSpec(memory_space=pl.ANY),
            pl.BlockSpec(memory_space=pltpu.HBM),
        ],
        out_specs=pl.BlockSpec(memory_space=pltpu.VMEM),
        scratch_shapes=[
            pltpu.VMEM((512, 4096), bf),
            pltpu.VMEM((2, 4, 4, 256, 512), bf),
            pltpu.VMEM((2, 2, 2, 256, 512), bf),
            pltpu.VMEM((2, 2, 4, 256, 512), bf),
            pltpu.VMEM((2, 4, 4, 64, 512), bf),
            pltpu.VMEM((2, 2, 2, 64, 512), bf),
            pltpu.VMEM((2, 2, 4, 64, 512), bf),
            pltpu.VMEM((2, 32, 4096), bf),
            pltpu.VMEM((32, 4096), bf),
            pltpu.VMEM((4, 256, 512), bf),
            pltpu.SemaphoreType.DMA((2, 2, 6)),
            pltpu.SemaphoreType.DMA((2, 2, 6)),
            pltpu.SemaphoreType.DMA,
            pltpu.SemaphoreType.DMA,
            pltpu.SemaphoreType.DMA((4,)),
        ],
        compiler_params=pltpu.CompilerParams(collective_id=2, has_side_effects=True, vmem_limit_bytes=48 * 2**20),
        cost_estimate=pl.CostEstimate(flops=2 * 1024 * 512 * 4096, bytes_accessed=10 * 2**20, transcendentals=0),
    )(tokens, slab, early, late)


def shards(weight_slab, token_rows, skew_params, pairing):
    early = lax.ppermute(partner_half(weight_slab), "tensor", [(d, d ^ 1) for d in range(32)])
    rotations = cayley_blocks(skew_params, pairing)
    tokens, late = turn_tokens(token_rows, rotations, weight_slab)
    return project(tokens, weight_slab, early, late)


def solution(mesh):
    in_specs = (
        P(("layer", "tensor"), None),
        P(("layer", "tensor"), None),
        P("layer", "tensor", None, None),
        P("layer", None),
    )
    out_specs = P(("layer", "tensor"), None)
    return jax.shard_map(shards, mesh=mesh, in_specs=in_specs, out_specs=out_specs, check_vma=False)
```

```python
import jax
import jax.numpy as jnp
import numpy as np
from jax import lax
from jax.experimental import pallas as pl
from jax.experimental.pallas import tpu as pltpu
from jax.sharding import PartitionSpec as P

HALF = 64
BLK = 128


def pair_table(distance, count):
    stride = 1 << distance
    rows = []
    for group in range(count // (2 * stride)):
        for offset in range(stride):
            low = group * 2 * stride + offset
            member = low if low >> 1 & 1 == 0 else low + stride
            rows.append((low, low + stride, (member >> 2) * 2 + (member & 1)))
    return rows


def split(value):
    high = value.astype(jnp.bfloat16)
    return high, (value - high.astype(jnp.float32)).astype(jnp.bfloat16)


def as_left(high, low):
    return jnp.concatenate([high, high, low], axis=1)


def as_right(high, low):
    return jnp.concatenate([high, low, high], axis=0)


def wide_dot(left, right):
    return jnp.dot(left, right, preferred_element_type=jnp.float32)


def full_dot(left, right):
    return jnp.dot(left, right, precision=lax.Precision.HIGHEST, preferred_element_type=jnp.float32)


def rotation_kernel(skew_ref, pairing_ref, out_ref, gram, gram_left, guess):
    count = gram.shape[0]
    rows = lax.broadcasted_iota(jnp.int32, (BLK, BLK), 0)
    lanes = lax.broadcasted_iota(jnp.int32, (BLK, BLK), 1)
    identity = (rows == lanes).astype(jnp.float32)
    largest = jnp.zeros((1, 1), jnp.float32)
    for block in range(count):
        raw = skew_ref[block]
        skewed = raw - raw.T
        square = full_dot(skewed, skewed)
        shifted = identity - square
        gram[block] = shifted
        gram_left[block] = as_left(*split(shifted))
        rounded = square.astype(jnp.bfloat16)
        fourth = jnp.dot(rounded, rounded, preferred_element_type=jnp.float32)
        largest = jnp.maximum(largest, jnp.sum(jnp.sum(fourth * fourth, axis=0, keepdims=True), axis=1, keepdims=True))
    top = 1.0 + 1.02 * jnp.sqrt(jnp.sqrt(0.5 * jnp.max(largest)))
    start = 2.0 / (1.0 + top)
    for block in range(count):
        guess[block] = identity * start

    def more(state):
        return state > 1e-2

    def improve(spread):
        shrunk = spread * spread / (2.0 - spread * spread)
        scale = 2.0 / (2.0 - spread * spread)
        for block in range(count):
            high, low = split(guess[block])
            left = 2.0 * identity - wide_dot(gram_left[block], as_right(high, low))
            guess[block] = scale * wide_dot(as_left(high, low), as_right(*split(left)))
        return shrunk

    lax.while_loop(more, improve, (top - 1.0) / (top + 1.0))
    for section in range(count // 2):
        turned = []
        for block in (2 * section, 2 * section + 1):
            raw = skew_ref[block]
            raised = identity + raw - raw.T
            now = guess[block]
            miss = identity - full_dot(gram[block], now)
            now = now + wide_dot(as_left(*split(now)), as_right(*split(miss)))
            rotation = 2.0 * wide_dot(as_left(*split(now)), as_right(*split(raised))) - identity
            turned.append(rotation.astype(jnp.bfloat16))
        order = pairing_ref[pl.ds(section, 1), :]
        chosen = (rows == order).astype(jnp.float32)
        inner = wide_dot(chosen.astype(jnp.bfloat16), jnp.concatenate(turned, axis=1)).astype(jnp.bfloat16)
        stacked = jnp.concatenate([inner[:, :BLK], inner[:, BLK:]], axis=0)
        outer = wide_dot(stacked, chosen.T.astype(jnp.bfloat16)).astype(jnp.bfloat16)
        out_ref[2 * section] = outer[:BLK]
        out_ref[2 * section + 1] = outer[BLK:]


def cayley_blocks(skew_params, pairing):
    sections, owned = skew_params.shape[:2]
    count = sections * owned
    out = pl.pallas_call(
        rotation_kernel,
        out_shape=jax.ShapeDtypeStruct((count, BLK, BLK), jnp.bfloat16),
        in_specs=[pl.BlockSpec(memory_space=pltpu.VMEM)] * 2,
        out_specs=pl.BlockSpec(memory_space=pltpu.VMEM),
        scratch_shapes=[
            pltpu.VMEM((count, BLK, BLK), jnp.float32),
            pltpu.VMEM((count, BLK, 3 * BLK), jnp.bfloat16),
            pltpu.VMEM((count, BLK, BLK), jnp.float32),
        ],
        cost_estimate=pl.CostEstimate(flops=count * BLK**3 * 20, bytes_accessed=count * BLK * BLK * 6, transcendentals=0),
    )(skew_params.reshape(count, BLK, BLK), pairing)
    return out.reshape(sections, owned, BLK, BLK)


def halves_dot(value, rotation_of, distance):
    halves = value.shape[1] // HALF
    parts = [None] * halves
    for low, high, owner in pair_table(distance, halves):
        joined = jnp.concatenate([value[:, low * HALF:(low + 1) * HALF], value[:, high * HALF:(high + 1) * HALF]], axis=1)
        turned = jnp.dot(joined, rotation_of(owner), preferred_element_type=jnp.float32).astype(jnp.bfloat16)
        parts[low], parts[high] = turned[:, :HALF], turned[:, HALF:]
    return jnp.concatenate(parts, axis=1)


def place():
    me = lax.axis_index("tensor")
    return me, me // 8, (me // 2) % 4, me % 2


def remote(src, dst, send, recv, peer):
    return pltpu.make_async_remote_copy(
        src_ref=src, dst_ref=dst, send_sem=send, recv_sem=recv,
        device_id={"tensor": peer}, device_id_type=pl.DeviceIdType.MESH,
    )


def greet(peers):
    barrier = pltpu.get_barrier_semaphore()
    for peer in peers:
        pl.semaphore_signal(barrier, inc=1, device_id={"tensor": peer}, device_id_type=pl.DeviceIdType.MESH)
    pl.semaphore_wait(barrier, len(peers))


def main_kernel(rows_ref, rot_ref, slab_ref, out_ref, rot_z, rot_x, rot_y, start, first, mid, second, third, landed, send_0, recv_0, send_e, recv_e, send_1, recv_1, send_2, recv_2, send_3, recv_3, send_4, recv_4, send_w, recv_w, own_w, tokens, slab, part, far, near, part2, far2, near2, last, swapped, send, recv, send_y, recv_y):
    me, z, x, y = place()
    spot = x * 2 + y
    own = pltpu.make_async_copy(slab_ref.at[:, pl.ds(pl.multiple_of(y * 4096, 4096), 4096)], slab.at[pl.ds(pl.multiple_of(y * 256, 256), 256)], own_w)
    own.start()
    partner = z * 8 + x * 2 + 1 - y
    greet([((z + step) % 4) * 8 + spot for step in range(1, 4)] + [z * 8 + (spot + step) % 8 for step in range(1, 8)])

    def gather(slot, source, target, peer):
        return remote(source, target, send_e.at[slot], recv_e.at[slot], peer)

    gathers_z = [gather(step - 1, rot_ref.at[pl.ds(4, 2)], rot_z.at[:, z], ((z + step) % 4) * 8 + spot) for step in (1, 3, 2)]
    gathers_x = [gather(2 + step, rot_ref.at[pl.ds(2, 2)], rot_x.at[:, x], z * 8 + ((x + step) % 4) * 2 + y) for step in (1, 3, 2)]
    gather_y = gather(6, rot_ref.at[pl.ds(0, 2)], rot_y.at[:, y], z * 8 + x * 2 + 1 - y)
    for copy in gathers_z:
        copy.start()

    def piece_of(other, group):
        at = pl.multiple_of(group * 2048 + other * 256, 256)
        return rows_ref.at[:, pl.ds(at, 256)]

    for step in range(1, 8):
        other = (spot + step) % 8
        for group in range(4):
            remote(piece_of(other, group), start.at[spot, :, pl.ds(group * 256, 256)], send_0.at[step], recv_0.at[spot], z * 8 + other).start()
    gather_y.start()

    columns = [(0, 1024), (2048, 512), (2560, 512), (1024, 1024), (3072, 1024)]
    rest = []
    for slot, (first_col, width) in enumerate(columns):
        source = slab_ref.at[:, pl.ds(pl.multiple_of((1 - y) * 4096 + first_col, 512), width)]
        target = slab.at[pl.ds(pl.multiple_of(y * 256, 256), 256), pl.ds(first_col, width)]
        rest.append(remote(source, target, send_w.at[slot], recv_w.at[slot], partner))
    rest[0].start()
    rest[1].start()
    for group in range(4):
        start[spot, :, group * 256:(group + 1) * 256] = rows_ref[:, pl.ds(pl.multiple_of(group * 2048 + spot * 256, 256), 256)]
    rot_z[:, z] = rot_ref[4:6]
    rot_x[:, x] = rot_ref[2:4]
    rot_y[:, y] = rot_ref[0:2]
    for step in range(1, 8):
        other = (spot + step) % 8
        remote(start.at[spot], start.at[other], send_0.at[step], recv_0.at[other], me).wait_recv()
    for copy in gathers_z:
        copy.wait_recv()
    for copy in gathers_x:
        copy.start()
    value = jnp.concatenate([start[other] for other in range(8)], axis=0)
    value = halves_dot(value, lambda k: rot_z[1, k // 2, k % 2], 3)
    value = halves_dot(value, lambda k: rot_z[0, k // 2, k % 2], 2)
    for piece in range(4):
        first[piece] = value[:, piece * 256:(piece + 1) * 256]

    over_z = [remote(first.at[(z + step) % 4], mid.at[z], send_1.at[step], recv_1.at[z], ((z + step) % 4) * 8 + spot) for step in (1, 3, 2)]
    for copy in over_z:
        copy.start()
    mid[z] = first[z]

    def onward(group):
        return remote(mid.at[group], second.at[x], send_2.at[group], recv_2.at[x], z * 8 + group * 2 + y)

    for step in (0, 3, 1, 2):
        group = (z + step) % 4
        if step != 0:
            remote(first.at[0], mid.at[group], send_1.at[step], recv_1.at[group], me).wait_recv()

        @pl.when(group != x)
        def _():
            onward(group).start()

        @pl.when(group == x)
        def _():
            second[x] = mid[group]

    for step in (1, 3, 2):
        source = (x + step) % 4
        remote(mid.at[0], second.at[source], send_2.at[0], recv_2.at[source], me).wait_recv()
    for copy in gathers_x:
        copy.wait_recv()
    value = jnp.concatenate([second[piece] for piece in range(4)], axis=1)
    value = halves_dot(value, lambda k: rot_x[1, k // 2, k % 2], 3)
    value = halves_dot(value, lambda k: rot_x[0, k // 2, k % 2], 2)
    for piece in range(4):
        third[piece] = value[:, piece * 256:(piece + 1) * 256]

    over_x = [remote(third.at[(x + step) % 4], landed.at[y, x], send_3.at[step], recv_3.at[x], z * 8 + ((x + step) % 4) * 2 + y) for step in (1, 3, 2)]
    for copy in over_x:
        copy.start()
    landed[y, x] = third[x]

    def across(group):
        return remote(landed.at[y, group], landed.at[y, group], send_4.at[group], recv_4.at[group], z * 8 + x * 2 + 1 - y)

    for step in (0, 3, 1, 2):
        group = (x + step) % 4
        if step != 0:
            remote(third.at[0], landed.at[y, group], send_3.at[step], recv_3.at[group], me).wait_recv()
        across(group).start()
    for copy in rest[2:]:
        copy.start()
    gather_y.wait_recv()
    for step in (0, 3, 1, 2):
        group = (x + step) % 4
        remote(landed.at[y, group], landed.at[1 - y, group], send_4.at[group], recv_4.at[group], me).wait_recv()
        value = jnp.concatenate([landed[0, group], landed[1, group]], axis=1)
        value = halves_dot(value, lambda k: rot_y[1, k // 2, k % 2], 2)
        value = halves_dot(value, lambda k: rot_y[0, k // 2, k % 2], 0)
        tokens[group] = value
    own.wait()

    coords = (z, x)

    def peer(axis, step):
        if axis == 0:
            return ((z + step) % 4) * 8 + spot
        return z * 8 + ((x + step) % 4) * 2 + y

    def compute(color, sub, role):
        block = (coords[color] + role) % 4
        if color == 0:
            left = tokens[block]
        else:
            left = jnp.concatenate([tokens[group, pl.ds(pl.multiple_of(block * 64, 64), 64), :] for group in range(4)], axis=0)

        def tile(half, carry):
            at = pl.multiple_of(color * 2048 + sub * 1024 + half * 512, 512)
            part[color, sub, role, half] = jnp.dot(left, slab[:, pl.ds(at, 512)], preferred_element_type=jnp.float32).astype(jnp.bfloat16)
            return carry

        lax.fori_loop(0, 2, tile, 0)

    pending = []

    def ship(stage, color, sub, slot, source, target, step):
        axis = color if stage == 0 else 1 - color
        copy = remote(source, target, send.at[stage, color, sub, slot], recv.at[stage, color, sub, slot], peer(axis, step))
        copy.start()
        pending.append(copy)
        return copy

    stages = ((part, far, near), (part2, far2, near2))
    fars, nears = {}, {}

    def start_far(stage, color, sub):
        block, far_buf, _ = stages[stage]
        fars[stage, color, sub] = (
            ship(stage, color, sub, 0, block.at[color, sub, 2, 0], far_buf.at[color, sub, 0], 1),
            ship(stage, color, sub, 1, block.at[color, sub, 2, 1], far_buf.at[color, sub, 1], 3),
        )

    def start_plain(stage, color, sub):
        block, _, near_buf = stages[stage]
        nears[stage, color, sub] = [
            ship(stage, color, sub, 2, block.at[color, sub, 1, 1], near_buf.at[color, sub, 0, 1], 1),
            ship(stage, color, sub, 3, block.at[color, sub, 3, 0], near_buf.at[color, sub, 1, 0], 3),
        ]

    def add(a, b):
        return (a.astype(jnp.float32) + b.astype(jnp.float32)).astype(jnp.bfloat16)

    def relay(stage, color, sub):
        block, far_buf, near_buf = stages[stage]
        fars[stage, color, sub][0].wait_recv()
        block[color, sub, 1, 0] = add(block[color, sub, 1, 0], far_buf[color, sub, 0])
        up = ship(stage, color, sub, 4, block.at[color, sub, 1, 0], near_buf.at[color, sub, 0, 0], 1)
        fars[stage, color, sub][1].wait_recv()
        block[color, sub, 3, 1] = add(block[color, sub, 3, 1], far_buf[color, sub, 1])
        down = ship(stage, color, sub, 5, block.at[color, sub, 3, 1], near_buf.at[color, sub, 1, 1], 3)
        nears[stage, color, sub] += [up, down]

    def second_stage(color, sub):
        for copy in nears[0, color, sub]:
            copy.wait_recv()
        for role in (2, 1, 3, 0):
            at = pl.ds(pl.multiple_of((coords[1 - color] + role) % 4 * 64, 64), 64)
            for half in range(2):
                total = part[color, sub, 0, half, at, :].astype(jnp.float32)
                total = total + near[color, sub, 0, half, at, :].astype(jnp.float32) + near[color, sub, 1, half, at, :].astype(jnp.float32)
                part2[color, sub, role, half] = total.astype(jnp.bfloat16)
            if role == 2:
                start_far(1, color, sub)
        start_plain(1, color, sub)

    def finish(color, sub):
        for copy in nears[1, color, sub]:
            copy.wait_recv()
        for half in range(2):
            total = part2[color, sub, 0, half].astype(jnp.float32)
            total = total + near2[color, sub, 0, half].astype(jnp.float32) + near2[color, sub, 1, half].astype(jnp.float32)
            total = total.astype(jnp.bfloat16)
            last[sub, 0, color, :, half * 512:half * 512 + 512] = total[:32]
            last[sub, 1, color, :, half * 512:half * 512 + 512] = total[32:]

    def first_stage(sub):
        for color in range(2):
            for slot in ((0,), (1, 2))[color] if sub == 0 else ((3,), (4,))[color]:
                width = columns[slot][1]
                there = slab.at[pl.ds(pl.multiple_of((1 - y) * 256, 256), 256), pl.ds(columns[slot][0], width)]
                remote(there, there, send_w.at[slot], recv_w.at[slot], me).wait_recv()
            compute(color, sub, 2)
            start_far(0, color, sub)
        for color in range(2):
            compute(color, sub, 1)
            compute(color, sub, 3)
            start_plain(0, color, sub)
        for color in range(2):
            compute(color, sub, 0)

    swaps = [remote(last.at[sub, 1 - y], swapped.at[sub], send_y.at[sub], recv_y.at[sub], partner) for sub in range(2)]

    def swap_out(sub):
        swaps[sub].start()
        for color in range(2):
            at = pl.multiple_of(y * 4096 + color * 2048 + sub * 1024, 1024)
            out_ref[:, pl.ds(at, 1024)] = last[sub, y, color]

    def swap_in(sub):
        swaps[sub].wait_recv()
        for color in range(2):
            at = pl.multiple_of((1 - y) * 4096 + color * 2048 + sub * 1024, 1024)
            out_ref[:, pl.ds(at, 1024)] = swapped[sub, color]

    first_stage(0)
    for color in range(2):
        relay(0, color, 0)
    first_stage(1)
    for color in range(2):
        second_stage(color, 0)
    for color in range(2):
        relay(0, color, 1)
    for color in range(2):
        relay(1, color, 0)
    for color in range(2):
        finish(color, 0)
    swap_out(0)
    for color in range(2):
        second_stage(color, 1)
    for color in range(2):
        relay(1, color, 1)
    for color in range(2):
        finish(color, 1)
    swap_out(1)
    swap_in(0)
    swap_in(1)
    for copy in swaps + pending:
        copy.wait_send()
    for copy in gathers_z + gathers_x + [gather_y] + rest + over_z + over_x:
        copy.wait_send()
    for step in range(1, 8):
        remote(start.at[spot], start.at[spot], send_0.at[step], recv_0.at[spot], me).wait_send()
    for group in range(4):
        across(group).wait_send()

        @pl.when(group != x)
        def _():
            onward(group).wait_send()


def rotate_and_project(rows, rotations, slab):
    bf = jnp.bfloat16
    dma = pltpu.SemaphoreType.DMA
    return pl.pallas_call(
        main_kernel,
        out_shape=jax.ShapeDtypeStruct((32, 8192), bf),
        in_specs=[pl.BlockSpec(memory_space=pltpu.VMEM)] * 2 + [pl.BlockSpec(memory_space=pl.ANY)],
        out_specs=pl.BlockSpec(memory_space=pltpu.VMEM),
        scratch_shapes=[
            pltpu.VMEM((2, 4, 2, BLK, BLK), bf),
            pltpu.VMEM((2, 4, 2, BLK, BLK), bf),
            pltpu.VMEM((2, 2, 2, BLK, BLK), bf),
            pltpu.VMEM((8, 32, 1024), bf),
            pltpu.VMEM((4, 256, 256), bf),
            pltpu.VMEM((4, 256, 256), bf),
            pltpu.VMEM((4, 256, 256), bf),
            pltpu.VMEM((4, 256, 256), bf),
            pltpu.VMEM((2, 4, 256, 256), bf),
        ]
        + [dma((count,)) for count in (8, 8, 7, 7, 4, 4, 4, 4, 4, 4, 4, 4, 5, 5)]
        + [
            dma,
            pltpu.VMEM((4, 256, 512), bf),
            pltpu.VMEM((512, 4096), bf),
            pltpu.VMEM((2, 2, 4, 2, 256, 512), bf),
            pltpu.VMEM((2, 2, 2, 256, 512), bf),
            pltpu.VMEM((2, 2, 2, 2, 256, 512), bf),
            pltpu.VMEM((2, 2, 4, 2, 64, 512), bf),
            pltpu.VMEM((2, 2, 2, 64, 512), bf),
            pltpu.VMEM((2, 2, 2, 2, 64, 512), bf),
            pltpu.VMEM((2, 2, 2, 32, 1024), bf),
            pltpu.VMEM((2, 2, 32, 1024), bf),
            dma((2, 2, 2, 6)),
            dma((2, 2, 2, 6)),
            dma((2,)),
            dma((2,)),
        ],
        compiler_params=pltpu.CompilerParams(collective_id=1, has_side_effects=True, vmem_limit_bytes=60 * 2**20),
        cost_estimate=pl.CostEstimate(flops=2 * 1024 * 512 * 4096, bytes_accessed=10 * 2**20, transcendentals=0),
    )(rows, rotations, slab)


def shards(weight_slab, token_rows, skew_params, pairing):
    return rotate_and_project(token_rows, cayley_blocks(skew_params, pairing), weight_slab)


def solution(mesh):
    in_specs = (
        P(("layer", "tensor"), None),
        P(("layer", "tensor"), None),
        P("layer", "tensor", None, None),
        P("layer", None),
    )
    out_specs = P(("layer", "tensor"), None)
    return jax.shard_map(shards, mesh=mesh, in_specs=in_specs, out_specs=out_specs, check_vma=False)
```

```python
import jax
import jax.numpy as jnp
import numpy as np
from jax import lax
from jax.experimental import pallas as pl
from jax.experimental.pallas import tpu as pltpu
from jax.sharding import PartitionSpec as P

HALF = 64
BLK = 128


def pair_table(distance, count):
    stride = 1 << distance
    rows = []
    for group in range(count // (2 * stride)):
        for offset in range(stride):
            low = group * 2 * stride + offset
            member = low if low >> 1 & 1 == 0 else low + stride
            rows.append((low, low + stride, (member >> 2) * 2 + (member & 1)))
    return rows


def split(value):
    high = value.astype(jnp.bfloat16)
    return high, (value - high.astype(jnp.float32)).astype(jnp.bfloat16)


def as_left(high, low):
    return jnp.concatenate([high, high, low], axis=1)


def as_right(high, low):
    return jnp.concatenate([high, low, high], axis=0)


def wide_dot(left, right):
    return jnp.dot(left, right, preferred_element_type=jnp.float32)


def full_dot(left, right):
    return jnp.dot(left, right, precision=lax.Precision.HIGHEST, preferred_element_type=jnp.float32)


def rotation_kernel(skew_ref, pairing_ref, out_ref, gram, gram_left, guess):
    count = gram.shape[0]
    rows = lax.broadcasted_iota(jnp.int32, (BLK, BLK), 0)
    lanes = lax.broadcasted_iota(jnp.int32, (BLK, BLK), 1)
    identity = (rows == lanes).astype(jnp.float32)
    largest = jnp.zeros((1, 1), jnp.float32)
    for block in range(count):
        raw = skew_ref[block]
        skewed = raw - raw.T
        square = full_dot(skewed, skewed)
        shifted = identity - square
        gram[block] = shifted
        gram_left[block] = as_left(*split(shifted))
        rounded = square.astype(jnp.bfloat16)
        fourth = jnp.dot(rounded, rounded, preferred_element_type=jnp.float32)
        largest = jnp.maximum(largest, jnp.sum(jnp.sum(fourth * fourth, axis=0, keepdims=True), axis=1, keepdims=True))
    top = 1.0 + 1.02 * jnp.sqrt(jnp.sqrt(0.5 * jnp.max(largest)))
    start = 2.0 / (1.0 + top)
    for block in range(count):
        guess[block] = identity * start

    def more(state):
        return state > 1e-2

    def improve(spread):
        shrunk = spread * spread / (2.0 - spread * spread)
        scale = 2.0 / (2.0 - spread * spread)
        for block in range(count):
            high, low = split(guess[block])
            left = 2.0 * identity - wide_dot(gram_left[block], as_right(high, low))
            guess[block] = scale * wide_dot(as_left(high, low), as_right(*split(left)))
        return shrunk

    lax.while_loop(more, improve, (top - 1.0) / (top + 1.0))
    for section in range(count // 2):
        turned = []
        for block in (2 * section, 2 * section + 1):
            raw = skew_ref[block]
            raised = identity + raw - raw.T
            now = guess[block]
            miss = identity - full_dot(gram[block], now)
            now = now + wide_dot(as_left(*split(now)), as_right(*split(miss)))
            rotation = 2.0 * wide_dot(as_left(*split(now)), as_right(*split(raised))) - identity
            turned.append(rotation.astype(jnp.bfloat16))
        order = pairing_ref[pl.ds(section, 1), :]
        chosen = (rows == order).astype(jnp.float32)
        inner = wide_dot(chosen.astype(jnp.bfloat16), jnp.concatenate(turned, axis=1)).astype(jnp.bfloat16)
        stacked = jnp.concatenate([inner[:, :BLK], inner[:, BLK:]], axis=0)
        outer = wide_dot(stacked, chosen.T.astype(jnp.bfloat16)).astype(jnp.bfloat16)
        out_ref[2 * section] = outer[:BLK]
        out_ref[2 * section + 1] = outer[BLK:]


def cayley_blocks(skew_params, pairing):
    sections, owned = skew_params.shape[:2]
    count = sections * owned
    out = pl.pallas_call(
        rotation_kernel,
        out_shape=jax.ShapeDtypeStruct((count, BLK, BLK), jnp.bfloat16),
        in_specs=[pl.BlockSpec(memory_space=pltpu.VMEM)] * 2,
        out_specs=pl.BlockSpec(memory_space=pltpu.VMEM),
        scratch_shapes=[
            pltpu.VMEM((count, BLK, BLK), jnp.float32),
            pltpu.VMEM((count, BLK, 3 * BLK), jnp.bfloat16),
            pltpu.VMEM((count, BLK, BLK), jnp.float32),
        ],
        cost_estimate=pl.CostEstimate(flops=count * BLK**3 * 20, bytes_accessed=count * BLK * BLK * 6, transcendentals=0),
    )(skew_params.reshape(count, BLK, BLK), pairing)
    return out.reshape(sections, owned, BLK, BLK)


def halves_dot(value, rotation_of, distance):
    halves = value.shape[1] // HALF
    parts = [None] * halves
    for low, high, owner in pair_table(distance, halves):
        joined = jnp.concatenate([value[:, low * HALF:(low + 1) * HALF], value[:, high * HALF:(high + 1) * HALF]], axis=1)
        turned = jnp.dot(joined, rotation_of(owner), preferred_element_type=jnp.float32).astype(jnp.bfloat16)
        parts[low], parts[high] = turned[:, :HALF], turned[:, HALF:]
    return jnp.concatenate(parts, axis=1)


def place():
    me = lax.axis_index("tensor")
    return me, me // 8, (me // 2) % 4, me % 2


def remote(src, dst, send, recv, peer):
    return pltpu.make_async_remote_copy(
        src_ref=src, dst_ref=dst, send_sem=send, recv_sem=recv,
        device_id={"tensor": peer}, device_id_type=pl.DeviceIdType.MESH,
    )


def greet(peers):
    barrier = pltpu.get_barrier_semaphore()
    for peer in peers:
        pl.semaphore_signal(barrier, inc=1, device_id={"tensor": peer}, device_id_type=pl.DeviceIdType.MESH)
    pl.semaphore_wait(barrier, len(peers))


def main_kernel(rows_ref, rot_ref, slab_ref, early_ref, out_ref, rot_z, rot_x, rot_y, start, first, mid, second, third, landed, send_0, recv_0, send_e, recv_e, send_1, recv_1, send_2, recv_2, send_3, recv_3, send_4, recv_4, send_w, recv_w, own_w, tokens, slab, part, far, near, merged, final, send, recv, send_f, recv_f, early_w):
    me, z, x, y = place()
    spot = x * 2 + y
    own = pltpu.make_async_copy(slab_ref.at[:, pl.ds(pl.multiple_of(y * 4096, 4096), 4096)], slab.at[pl.ds(pl.multiple_of(y * 256, 256), 256)], own_w)
    own.start()
    early = pltpu.make_async_copy(early_ref, slab.at[pl.ds(pl.multiple_of((1 - y) * 256, 256), 256), pl.ds(0, 1024)], early_w)
    early.start()
    partner = z * 8 + x * 2 + 1 - y
    greet([((z + step) % 4) * 8 + spot for step in range(1, 4)] + [z * 8 + (spot + step) % 8 for step in range(1, 8)] + [((z + step) % 4) * 8 + x * 2 + 1 - y for step in range(1, 4)])

    def gather(slot, source, target, peer):
        return remote(source, target, send_e.at[slot], recv_e.at[slot], peer)

    gathers_z = [gather(step - 1, rot_ref.at[pl.ds(4, 2)], rot_z.at[:, z], ((z + step) % 4) * 8 + spot) for step in (1, 3, 2)]
    gathers_x = [gather(2 + step, rot_ref.at[pl.ds(2, 2)], rot_x.at[:, x], z * 8 + ((x + step) % 4) * 2 + y) for step in (1, 3, 2)]
    gather_y = gather(6, rot_ref.at[pl.ds(0, 2)], rot_y.at[:, y], z * 8 + x * 2 + 1 - y)
    for copy in gathers_z:
        copy.start()

    def piece_of(other, group):
        at = pl.multiple_of(group * 2048 + other * 256, 256)
        return rows_ref.at[:, pl.ds(at, 256)]

    for step in range(1, 8):
        other = (spot + step) % 8
        for group in range(4):
            remote(piece_of(other, group), start.at[spot, :, pl.ds(group * 256, 256)], send_0.at[step], recv_0.at[spot], z * 8 + other).start()
    gather_y.start()

    columns = [(1024, 1024), (2048, 1024), (3072, 1024)]
    rest = []
    for slot, (first_col, width) in enumerate(columns):
        source = slab_ref.at[:, pl.ds(pl.multiple_of((1 - y) * 4096 + first_col, 512), width)]
        target = slab.at[pl.ds(pl.multiple_of(y * 256, 256), 256), pl.ds(first_col, width)]
        rest.append(remote(source, target, send_w.at[slot], recv_w.at[slot], partner))
    rest[0].start()
    for group in range(4):
        start[spot, :, group * 256:(group + 1) * 256] = rows_ref[:, pl.ds(pl.multiple_of(group * 2048 + spot * 256, 256), 256)]
    rot_z[:, z] = rot_ref[4:6]
    rot_x[:, x] = rot_ref[2:4]
    rot_y[:, y] = rot_ref[0:2]
    for step in range(1, 8):
        other = (spot + step) % 8
        remote(start.at[spot], start.at[other], send_0.at[step], recv_0.at[other], me).wait_recv()
    for copy in gathers_z:
        copy.wait_recv()
    for copy in gathers_x:
        copy.start()
    value = jnp.concatenate([start[other] for other in range(8)], axis=0)
    value = halves_dot(value, lambda k: rot_z[1, k // 2, k % 2], 3)
    value = halves_dot(value, lambda k: rot_z[0, k // 2, k % 2], 2)
    for piece in range(4):
        first[piece] = value[:, piece * 256:(piece + 1) * 256]

    over_z = [remote(first.at[(z + step) % 4], mid.at[z], send_1.at[step], recv_1.at[z], ((z + step) % 4) * 8 + spot) for step in (1, 3, 2)]
    for copy in over_z:
        copy.start()
    mid[z] = first[z]

    def onward(group):
        return remote(mid.at[group], second.at[x], send_2.at[group], recv_2.at[x], z * 8 + group * 2 + y)

    for step in (0, 3, 1, 2):
        group = (z + step) % 4
        if step != 0:
            remote(first.at[0], mid.at[group], send_1.at[step], recv_1.at[group], me).wait_recv()

        @pl.when(group != x)
        def _():
            onward(group).start()

        @pl.when(group == x)
        def _():
            second[x] = mid[group]

    for step in (1, 3, 2):
        source = (x + step) % 4
        remote(mid.at[0], second.at[source], send_2.at[0], recv_2.at[source], me).wait_recv()
    for copy in gathers_x:
        copy.wait_recv()
    value = jnp.concatenate([second[piece] for piece in range(4)], axis=1)
    value = halves_dot(value, lambda k: rot_x[1, k // 2, k % 2], 3)
    value = halves_dot(value, lambda k: rot_x[0, k // 2, k % 2], 2)
    for piece in range(4):
        third[piece] = value[:, piece * 256:(piece + 1) * 256]

    over_x = [remote(third.at[(x + step) % 4], landed.at[y, x], send_3.at[step], recv_3.at[x], z * 8 + ((x + step) % 4) * 2 + y) for step in (1, 3, 2)]
    for copy in over_x:
        copy.start()
    landed[y, x] = third[x]

    def across(group):
        return remote(landed.at[y, group], landed.at[y, group], send_4.at[group], recv_4.at[group], z * 8 + x * 2 + 1 - y)

    for step in (0, 3, 1, 2):
        group = (x + step) % 4
        if step != 0:
            remote(third.at[0], landed.at[y, group], send_3.at[step], recv_3.at[group], me).wait_recv()
        across(group).start()
    for copy in rest[1:]:
        copy.start()
    gather_y.wait_recv()
    for step in (0, 3, 1, 2):
        group = (x + step) % 4
        remote(landed.at[y, group], landed.at[1 - y, group], send_4.at[group], recv_4.at[group], me).wait_recv()
        value = jnp.concatenate([landed[0, group], landed[1, group]], axis=1)
        value = halves_dot(value, lambda k: rot_y[1, k // 2, k % 2], 2)
        value = halves_dot(value, lambda k: rot_y[0, k // 2, k % 2], 0)
        tokens[group] = value
    own.wait()
    early.wait()

    coords = (z, x)

    def peer(axis, step):
        if axis == 0:
            return ((z + step) % 4) * 8 + spot
        return z * 8 + ((x + step) % 4) * 2 + y

    def compute(color, sub, role):
        block = (coords[color] + role) % 4
        if color == 0:
            left = tokens[block]
        else:
            left = jnp.concatenate([tokens[group, pl.ds(pl.multiple_of(block * 64, 64), 64), :] for group in range(4)], axis=0)

        def tile(half, carry):
            at = pl.multiple_of(sub * 2048 + color * 1024 + half * 512, 512)
            part[color, sub, role, half] = jnp.dot(left, slab[:, pl.ds(at, 512)], preferred_element_type=jnp.float32).astype(jnp.bfloat16)
            return carry

        lax.fori_loop(0, 2, tile, 0)

    pending = []

    def ship(color, sub, slot, source, target, step):
        copy = remote(source, target, send.at[color, sub, slot], recv.at[color, sub, slot], peer(color, step))
        copy.start()
        pending.append(copy)
        return copy

    fars, nears = {}, {}

    def start_far(color, sub):
        fars[color, sub] = (
            ship(color, sub, 0, part.at[color, sub, 2, 0], far.at[color, sub, 0], 1),
            ship(color, sub, 1, part.at[color, sub, 2, 1], far.at[color, sub, 1], 3),
        )

    def start_plain(color, sub):
        nears[color, sub] = [
            ship(color, sub, 2, part.at[color, sub, 1, 1], near.at[color, sub, 0, 1], 1),
            ship(color, sub, 3, part.at[color, sub, 3, 0], near.at[color, sub, 1, 0], 3),
        ]

    def add(a, b):
        return (a.astype(jnp.float32) + b.astype(jnp.float32)).astype(jnp.bfloat16)

    def relay(color, sub):
        fars[color, sub][0].wait_recv()
        part[color, sub, 1, 0] = add(part[color, sub, 1, 0], far[color, sub, 0])
        up = ship(color, sub, 4, part.at[color, sub, 1, 0], near.at[color, sub, 0, 0], 1)
        fars[color, sub][1].wait_recv()
        part[color, sub, 3, 1] = add(part[color, sub, 3, 1], far[color, sub, 1])
        down = ship(color, sub, 5, part.at[color, sub, 3, 1], near.at[color, sub, 1, 1], 3)
        nears[color, sub] += [up, down]

    def owner(color, step, cross):
        side = 1 - y if cross else y
        if color == 0:
            return z * 8 + ((x + step) % 4) * 2 + side
        return ((z + step) % 4) * 8 + x * 2 + side

    def second_stage(color, sub):
        for copy in nears[color, sub]:
            copy.wait_recv()
        here = coords[1 - color]
        for step in (2, 1, 3, 0):
            there = (here + step) % 4
            at = pl.ds(pl.multiple_of(there * 64, 64), 64)
            for half in range(2):
                total = part[color, sub, 0, half, at, :].astype(jnp.float32)
                total = total + near[color, sub, 0, half, at, :].astype(jnp.float32) + near[color, sub, 1, half, at, :].astype(jnp.float32)
                total = total.astype(jnp.bfloat16)
                merged[color, sub, step, 0, :, half * 512:half * 512 + 512] = total[:32]
                merged[color, sub, step, 1, :, half * 512:half * 512 + 512] = total[32:]
            for cross in (1, 0):
                if step != 0 or cross == 1:
                    side = 1 - y if cross else y
                    slot = step * 2 + cross
                    copy = remote(merged.at[color, sub, step, side], final.at[color, sub, slot], send_f.at[color, sub, slot], recv_f.at[color, sub, slot], owner(color, step, cross))
                    copy.start()
                    pending.append(copy)

    def finish(color, sub):
        for cross in (0, 1):
            total = jnp.zeros((32, 1024), jnp.float32)
            if cross == 0:
                total = merged[color, sub, 0, y].astype(jnp.float32)
            for step in (0, 1, 3, 2):
                slot = step * 2 + cross
                if slot != 0:
                    landing = final.at[color, sub, slot]
                    remote(landing, landing, send_f.at[color, sub, slot], recv_f.at[color, sub, slot], me).wait_recv()
                    total = total + final[color, sub, slot].astype(jnp.float32)
            side = 1 - y if cross else y
            at = pl.multiple_of(side * 4096 + sub * 2048 + color * 1024, 1024)
            out_ref[:, pl.ds(at, 1024)] = total.astype(jnp.bfloat16)

    def arrived(slot):
        there = slab.at[pl.ds(pl.multiple_of((1 - y) * 256, 256), 256), pl.ds(columns[slot][0], columns[slot][1])]
        remote(there, there, send_w.at[slot], recv_w.at[slot], me).wait_recv()

    compute(0, 0, 2)
    start_far(0, 0)
    arrived(0)
    compute(1, 0, 2)
    start_far(1, 0)
    for color in range(2):
        compute(color, 0, 1)
        compute(color, 0, 3)
        start_plain(color, 0)
    for color in range(2):
        compute(color, 0, 0)
    for color in range(2):
        relay(color, 0)
    arrived(1)
    compute(0, 1, 2)
    start_far(0, 1)
    compute(0, 1, 1)
    compute(0, 1, 3)
    start_plain(0, 1)
    compute(0, 1, 0)
    arrived(2)
    compute(1, 1, 2)
    start_far(1, 1)
    compute(1, 1, 1)
    compute(1, 1, 3)
    start_plain(1, 1)
    compute(1, 1, 0)
    for color in range(2):
        second_stage(color, 0)
    for color in range(2):
        relay(color, 1)
    for color in range(2):
        finish(color, 0)
    for color in range(2):
        second_stage(color, 1)
    for color in range(2):
        finish(color, 1)
    for copy in pending:
        copy.wait_send()
    for copy in gathers_z + gathers_x + [gather_y] + rest + over_z + over_x:
        copy.wait_send()
    for step in range(1, 8):
        remote(start.at[spot], start.at[spot], send_0.at[step], recv_0.at[spot], me).wait_send()
    for group in range(4):
        across(group).wait_send()

        @pl.when(group != x)
        def _():
            onward(group).wait_send()


def rotate_and_project(rows, rotations, slab, early):
    bf = jnp.bfloat16
    dma = pltpu.SemaphoreType.DMA
    return pl.pallas_call(
        main_kernel,
        out_shape=jax.ShapeDtypeStruct((32, 8192), bf),
        in_specs=[pl.BlockSpec(memory_space=pltpu.VMEM)] * 2 + [pl.BlockSpec(memory_space=pl.ANY)] * 2,
        out_specs=pl.BlockSpec(memory_space=pltpu.VMEM),
        scratch_shapes=[
            pltpu.VMEM((2, 4, 2, BLK, BLK), bf),
            pltpu.VMEM((2, 4, 2, BLK, BLK), bf),
            pltpu.VMEM((2, 2, 2, BLK, BLK), bf),
            pltpu.VMEM((8, 32, 1024), bf),
            pltpu.VMEM((4, 256, 256), bf),
            pltpu.VMEM((4, 256, 256), bf),
            pltpu.VMEM((4, 256, 256), bf),
            pltpu.VMEM((4, 256, 256), bf),
            pltpu.VMEM((2, 4, 256, 256), bf),
        ]
        + [dma((count,)) for count in (8, 8, 7, 7, 4, 4, 4, 4, 4, 4, 4, 4, 3, 3)]
        + [
            dma,
            pltpu.VMEM((4, 256, 512), bf),
            pltpu.VMEM((512, 4096), bf),
            pltpu.VMEM((2, 2, 4, 2, 256, 512), bf),
            pltpu.VMEM((2, 2, 2, 256, 512), bf),
            pltpu.VMEM((2, 2, 2, 2, 256, 512), bf),
            pltpu.VMEM((2, 2, 4, 2, 32, 1024), bf),
            pltpu.VMEM((2, 2, 8, 32, 1024), bf),
            dma((2, 2, 6)),
            dma((2, 2, 6)),
            dma((2, 2, 8)),
            dma((2, 2, 8)),
            dma,
        ],
        compiler_params=pltpu.CompilerParams(collective_id=1, has_side_effects=True, vmem_limit_bytes=52 * 2**20),
        cost_estimate=pl.CostEstimate(flops=2 * 1024 * 512 * 4096, bytes_accessed=10 * 2**20, transcendentals=0),
    )(rows, rotations, slab, early)


def half_kernel(slab_ref, out_ref, done):
    side = lax.axis_index("tensor") % 2
    at = pl.multiple_of((1 - side) * 4096, 4096)
    copy = pltpu.make_async_copy(slab_ref.at[:, pl.ds(at, 1024)], out_ref, done)
    copy.start()
    copy.wait()


def partner_columns(slab):
    return pl.pallas_call(
        half_kernel,
        out_shape=jax.ShapeDtypeStruct((256, 1024), jnp.bfloat16),
        in_specs=[pl.BlockSpec(memory_space=pl.ANY)],
        out_specs=pl.BlockSpec(memory_space=pltpu.VMEM),
        scratch_shapes=[pltpu.SemaphoreType.DMA],
        cost_estimate=pl.CostEstimate(flops=0, bytes_accessed=4 * 2**20, transcendentals=0),
    )(slab)


def shards(weight_slab, token_rows, skew_params, pairing):
    early = lax.ppermute(partner_columns(weight_slab), "tensor", [(d, d ^ 1) for d in range(32)])
    return rotate_and_project(token_rows, cayley_blocks(skew_params, pairing), weight_slab, early)


def solution(mesh):
    in_specs = (
        P(("layer", "tensor"), None),
        P(("layer", "tensor"), None),
        P("layer", "tensor", None, None),
        P("layer", None),
    )
    out_specs = P(("layer", "tensor"), None)
    return jax.shard_map(shards, mesh=mesh, in_specs=in_specs, out_specs=out_specs, check_vma=False)
```

```python
import jax
import jax.numpy as jnp
import numpy as np
from jax import lax
from jax.experimental import pallas as pl
from jax.experimental.pallas import tpu as pltpu
from jax.sharding import PartitionSpec as P

HALF = 64
BLK = 128


def pair_table(distance, count):
    stride = 1 << distance
    rows = []
    for group in range(count // (2 * stride)):
        for offset in range(stride):
            low = group * 2 * stride + offset
            member = low if low >> 1 & 1 == 0 else low + stride
            rows.append((low, low + stride, (member >> 2) * 2 + (member & 1)))
    return rows


def split(value):
    high = value.astype(jnp.bfloat16)
    return high, (value - high.astype(jnp.float32)).astype(jnp.bfloat16)


def as_left(high, low):
    return jnp.concatenate([high, low], axis=1)


def as_right(high, low):
    row = jnp.concatenate([high, low], axis=1)
    return jnp.concatenate([row, row], axis=0)


def wide_dot(left, right):
    return jnp.dot(left, right, preferred_element_type=jnp.float32)


def folded_dot(left, right):
    both = wide_dot(left, right)
    return both[:, :BLK] + both[:, BLK:]


def split_three(value):
    high = value.astype(jnp.bfloat16)
    left_over = value - high.astype(jnp.float32)
    middle = left_over.astype(jnp.bfloat16)
    return high, middle, (left_over - middle.astype(jnp.float32)).astype(jnp.bfloat16)


def full_dot(left, right):
    left_hi, left_mid, left_lo = split_three(left)
    right_hi, right_mid, right_lo = split_three(right)
    small = wide_dot(as_left(left_hi, left_lo), jnp.concatenate([right_lo, right_hi], axis=0))
    return folded_dot(as_left(left_hi, left_mid), as_right(right_hi, right_mid)) + small


def rotation_kernel(skew_ref, pairing_ref, out_ref, gram, gram_left, guess):
    count = gram.shape[0]
    rows = lax.broadcasted_iota(jnp.int32, (BLK, BLK), 0)
    lanes = lax.broadcasted_iota(jnp.int32, (BLK, BLK), 1)
    identity = (rows == lanes).astype(jnp.float32)
    largest = jnp.zeros((1, 1), jnp.float32)
    for block in range(count):
        raw = skew_ref[block]
        skewed = raw - raw.T
        square = full_dot(skewed, skewed)
        shifted = identity - square
        gram[block] = shifted
        gram_left[block] = as_left(*split(shifted))
        rounded = square.astype(jnp.bfloat16)
        fourth = jnp.dot(rounded, rounded, preferred_element_type=jnp.float32)
        largest = jnp.maximum(largest, jnp.sum(jnp.sum(fourth * fourth, axis=0, keepdims=True), axis=1, keepdims=True))
    top = 1.0 + 1.02 * jnp.sqrt(jnp.sqrt(0.5 * jnp.max(largest)))
    start = 2.0 / (1.0 + top)
    for block in range(count):
        guess[block] = identity * start

    def more(state):
        return state > 1e-2

    def improve(spread):
        shrunk = spread * spread / (2.0 - spread * spread)
        scale = 2.0 / (2.0 - spread * spread)
        for block in range(count):
            high, low = split(guess[block])
            left = 2.0 * identity - folded_dot(gram_left[block], as_right(high, low))
            guess[block] = scale * folded_dot(as_left(high, low), as_right(*split(left)))
        return shrunk

    lax.while_loop(more, improve, (top - 1.0) / (top + 1.0))
    for section in range(count // 2):
        turned = []
        for block in (2 * section, 2 * section + 1):
            raw = skew_ref[block]
            raised = identity + raw - raw.T
            now = guess[block]
            miss = identity - full_dot(gram[block], now)
            now = now + folded_dot(as_left(*split(now)), as_right(*split(miss)))
            rotation = 2.0 * folded_dot(as_left(*split(now)), as_right(*split(raised))) - identity
            turned.append(rotation.astype(jnp.bfloat16))
        order = pairing_ref[pl.ds(section, 1), :]
        chosen = (rows == order).astype(jnp.float32)
        inner = wide_dot(chosen.astype(jnp.bfloat16), jnp.concatenate(turned, axis=1)).astype(jnp.bfloat16)
        stacked = jnp.concatenate([inner[:, :BLK], inner[:, BLK:]], axis=0)
        outer = wide_dot(stacked, chosen.T.astype(jnp.bfloat16)).astype(jnp.bfloat16)
        out_ref[2 * section] = outer[:BLK]
        out_ref[2 * section + 1] = outer[BLK:]


def cayley_blocks(skew_params, pairing):
    sections, owned = skew_params.shape[:2]
    count = sections * owned
    out = pl.pallas_call(
        rotation_kernel,
        out_shape=jax.ShapeDtypeStruct((count, BLK, BLK), jnp.bfloat16),
        in_specs=[pl.BlockSpec(memory_space=pltpu.VMEM)] * 2,
        out_specs=pl.BlockSpec(memory_space=pltpu.VMEM),
        scratch_shapes=[
            pltpu.VMEM((count, BLK, BLK), jnp.float32),
            pltpu.VMEM((count, BLK, 2 * BLK), jnp.bfloat16),
            pltpu.VMEM((count, BLK, BLK), jnp.float32),
        ],
        compiler_params=pltpu.CompilerParams(vmem_limit_bytes=16 * 2**20),
        cost_estimate=pl.CostEstimate(flops=count * BLK**3 * 20, bytes_accessed=count * BLK * BLK * 6, transcendentals=0),
    )(skew_params.reshape(count, BLK, BLK), pairing)
    return out.reshape(sections, owned, BLK, BLK)


def halves_dot(value, rotation_of, distance):
    halves = value.shape[1] // HALF
    parts = [None] * halves
    for low, high, owner in pair_table(distance, halves):
        joined = jnp.concatenate([value[:, low * HALF:(low + 1) * HALF], value[:, high * HALF:(high + 1) * HALF]], axis=1)
        turned = jnp.dot(joined, rotation_of(owner), preferred_element_type=jnp.float32).astype(jnp.bfloat16)
        parts[low], parts[high] = turned[:, :HALF], turned[:, HALF:]
    return jnp.concatenate(parts, axis=1)


def place():
    me = lax.axis_index("tensor")
    return me, me // 8, (me // 2) % 4, me % 2


def remote(src, dst, send, recv, peer):
    return pltpu.make_async_remote_copy(
        src_ref=src, dst_ref=dst, send_sem=send, recv_sem=recv,
        device_id={"tensor": peer}, device_id_type=pl.DeviceIdType.MESH,
    )


def greet(peers):
    barrier = pltpu.get_barrier_semaphore()
    for peer in peers:
        pl.semaphore_signal(barrier, inc=1, device_id={"tensor": peer}, device_id_type=pl.DeviceIdType.MESH)
    pl.semaphore_wait(barrier, len(peers))


def main_kernel(rows_ref, rot_ref, slab_ref, early_ref, out_ref, rot_z, rot_x, rot_y, start, first, mid, second, third, landed, send_0, recv_0, send_e, recv_e, send_1, recv_1, send_2, recv_2, send_3, recv_3, send_4, recv_4, send_w, recv_w, own_w, tokens, slab, part, far, near, merged, final, send, recv, send_f, recv_f, early_w):
    me, z, x, y = place()
    spot = x * 2 + y
    own = pltpu.make_async_copy(slab_ref.at[:, pl.ds(pl.multiple_of(y * 4096, 4096), 4096)], slab.at[pl.ds(pl.multiple_of(y * 256, 256), 256)], own_w)
    own.start()
    early = pltpu.make_async_copy(early_ref, slab.at[pl.ds(pl.multiple_of((1 - y) * 256, 256), 256), pl.ds(0, 768)], early_w)
    early.start()
    partner = z * 8 + x * 2 + 1 - y
    greet([((z + step) % 4) * 8 + spot for step in range(1, 4)] + [z * 8 + (spot + step) % 8 for step in range(1, 8)] + [((z + step) % 4) * 8 + x * 2 + 1 - y for step in range(1, 4)])

    def gather(slot, source, target, peer):
        return remote(source, target, send_e.at[slot], recv_e.at[slot], peer)

    gathers_z = [gather(step - 1, rot_ref.at[pl.ds(4, 2)], rot_z.at[:, z], ((z + step) % 4) * 8 + spot) for step in (1, 3, 2)]
    gathers_x = [gather(2 + step, rot_ref.at[pl.ds(2, 2)], rot_x.at[:, x], z * 8 + ((x + step) % 4) * 2 + y) for step in (1, 3, 2)]
    gather_y = gather(6, rot_ref.at[pl.ds(0, 2)], rot_y.at[:, y], z * 8 + x * 2 + 1 - y)
    for copy in gathers_z:
        copy.start()

    def piece_of(other, group):
        at = pl.multiple_of(group * 2048 + other * 256, 256)
        return rows_ref.at[:, pl.ds(at, 256)]

    for step in range(1, 8):
        other = (spot + step) % 8
        for group in range(4):
            remote(piece_of(other, group), start.at[spot, :, pl.ds(group * 256, 256)], send_0.at[step], recv_0.at[spot], z * 8 + other).start()
    gather_y.start()

    columns = [(768, 1280), (2048, 1024), (3072, 1024)]
    rest = []
    for slot, (first_col, width) in enumerate(columns):
        source = slab_ref.at[:, pl.ds(pl.multiple_of((1 - y) * 4096 + first_col, 256), width)]
        target = slab.at[pl.ds(pl.multiple_of(y * 256, 256), 256), pl.ds(first_col, width)]
        rest.append(remote(source, target, send_w.at[slot], recv_w.at[slot], partner))
    rest[0].start()
    for group in range(4):
        start[spot, :, group * 256:(group + 1) * 256] = rows_ref[:, pl.ds(pl.multiple_of(group * 2048 + spot * 256, 256), 256)]
    rot_z[:, z] = rot_ref[4:6]
    rot_x[:, x] = rot_ref[2:4]
    rot_y[:, y] = rot_ref[0:2]
    for step in range(1, 8):
        other = (spot + step) % 8
        remote(start.at[spot], start.at[other], send_0.at[step], recv_0.at[other], me).wait_recv()
    for copy in gathers_z:
        copy.wait_recv()
    for copy in gathers_x:
        copy.start()
    value = jnp.concatenate([start[other] for other in range(8)], axis=0)
    value = halves_dot(value, lambda k: rot_z[1, k // 2, k % 2], 3)
    value = halves_dot(value, lambda k: rot_z[0, k // 2, k % 2], 2)
    for piece in range(4):
        first[piece] = value[:, piece * 256:(piece + 1) * 256]

    over_z = [remote(first.at[(z + step) % 4], mid.at[z], send_1.at[step], recv_1.at[z], ((z + step) % 4) * 8 + spot) for step in (1, 3, 2)]
    for copy in over_z:
        copy.start()
    mid[z] = first[z]

    def onward(group):
        return remote(mid.at[group], second.at[x], send_2.at[group], recv_2.at[x], z * 8 + group * 2 + y)

    for step in (0, 3, 1, 2):
        group = (z + step) % 4
        if step != 0:
            remote(first.at[0], mid.at[group], send_1.at[step], recv_1.at[group], me).wait_recv()

        @pl.when(group != x)
        def _():
            onward(group).start()

        @pl.when(group == x)
        def _():
            second[x] = mid[group]

    for step in (1, 3, 2):
        source = (x + step) % 4
        remote(mid.at[0], second.at[source], send_2.at[0], recv_2.at[source], me).wait_recv()
    for copy in gathers_x:
        copy.wait_recv()
    value = jnp.concatenate([second[piece] for piece in range(4)], axis=1)
    value = halves_dot(value, lambda k: rot_x[1, k // 2, k % 2], 3)
    value = halves_dot(value, lambda k: rot_x[0, k // 2, k % 2], 2)
    for piece in range(4):
        third[piece] = value[:, piece * 256:(piece + 1) * 256]

    over_x = [remote(third.at[(x + step) % 4], landed.at[y, x], send_3.at[step], recv_3.at[x], z * 8 + ((x + step) % 4) * 2 + y) for step in (1, 3, 2)]
    for copy in over_x:
        copy.start()
    landed[y, x] = third[x]

    def across(group):
        return remote(landed.at[y, group], landed.at[y, group], send_4.at[group], recv_4.at[group], z * 8 + x * 2 + 1 - y)

    for step in (0, 3, 1, 2):
        group = (x + step) % 4
        if step != 0:
            remote(third.at[0], landed.at[y, group], send_3.at[step], recv_3.at[group], me).wait_recv()
        across(group).start()
    for copy in rest[1:]:
        copy.start()
    gather_y.wait_recv()
    for step in (0, 3, 1, 2):
        group = (x + step) % 4
        remote(landed.at[y, group], landed.at[1 - y, group], send_4.at[group], recv_4.at[group], me).wait_recv()
        value = jnp.concatenate([landed[0, group], landed[1, group]], axis=1)
        value = halves_dot(value, lambda k: rot_y[1, k // 2, k % 2], 2)
        value = halves_dot(value, lambda k: rot_y[0, k // 2, k % 2], 0)
        tokens[group] = value
    own.wait()
    early.wait()

    coords = (z, x)

    def peer(axis, step):
        if axis == 0:
            return ((z + step) % 4) * 8 + spot
        return z * 8 + ((x + step) % 4) * 2 + y

    def compute(color, sub, role):
        block = (coords[color] + role) % 4
        if color == 0:
            left = tokens[block]
        else:
            left = jnp.concatenate([tokens[group, pl.ds(pl.multiple_of(block * 64, 64), 64), :] for group in range(4)], axis=0)

        def tile(half, carry):
            at = pl.multiple_of(sub * 2048 + color * 1024 + half * 512, 512)
            part[color, sub, role, half] = jnp.dot(left, slab[:, pl.ds(at, 512)], preferred_element_type=jnp.float32).astype(jnp.bfloat16)
            return carry

        lax.fori_loop(0, 2, tile, 0)

    pending = []

    def ship(color, sub, slot, source, target, step):
        copy = remote(source, target, send.at[color, sub, slot], recv.at[color, sub, slot], peer(color, step))
        copy.start()
        pending.append(copy)
        return copy

    fars, nears = {}, {}

    def start_far(color, sub):
        fars[color, sub] = (
            ship(color, sub, 0, part.at[color, sub, 2, 0], far.at[color, sub, 0], 1),
            ship(color, sub, 1, part.at[color, sub, 2, 1], far.at[color, sub, 1], 3),
        )

    def start_plain(color, sub):
        nears[color, sub] = [
            ship(color, sub, 2, part.at[color, sub, 1, 1], near.at[color, sub, 0, 1], 1),
            ship(color, sub, 3, part.at[color, sub, 3, 0], near.at[color, sub, 1, 0], 3),
        ]

    def add(a, b):
        return (a.astype(jnp.float32) + b.astype(jnp.float32)).astype(jnp.bfloat16)

    def relay(color, sub):
        fars[color, sub][0].wait_recv()
        part[color, sub, 1, 0] = add(part[color, sub, 1, 0], far[color, sub, 0])
        up = ship(color, sub, 4, part.at[color, sub, 1, 0], near.at[color, sub, 0, 0], 1)
        fars[color, sub][1].wait_recv()
        part[color, sub, 3, 1] = add(part[color, sub, 3, 1], far[color, sub, 1])
        down = ship(color, sub, 5, part.at[color, sub, 3, 1], near.at[color, sub, 1, 1], 3)
        nears[color, sub] += [up, down]

    def owner(color, step, cross):
        side = 1 - y if cross else y
        if color == 0:
            return z * 8 + ((x + step) % 4) * 2 + side
        return ((z + step) % 4) * 8 + x * 2 + side

    def second_stage(color, sub):
        for copy in nears[color, sub]:
            copy.wait_recv()
        here = coords[1 - color]
        for step in (2, 1, 3, 0):
            there = (here + step) % 4
            at = pl.ds(pl.multiple_of(there * 64, 64), 64)
            for half in range(2):
                total = part[color, sub, 0, half, at, :].astype(jnp.float32)
                total = total + near[color, sub, 0, half, at, :].astype(jnp.float32) + near[color, sub, 1, half, at, :].astype(jnp.float32)
                total = total.astype(jnp.bfloat16)
                merged[color, sub, step, 0, :, half * 512:half * 512 + 512] = total[:32]
                merged[color, sub, step, 1, :, half * 512:half * 512 + 512] = total[32:]
            for cross in (1, 0):
                if step != 0 or cross == 1:
                    side = 1 - y if cross else y
                    slot = step * 2 + cross
                    copy = remote(merged.at[color, sub, step, side], final.at[color, sub, slot], send_f.at[color, sub, slot], recv_f.at[color, sub, slot], owner(color, step, cross))
                    copy.start()
                    pending.append(copy)

    def finish(color, sub):
        for cross in (0, 1):
            total = jnp.zeros((32, 1024), jnp.float32)
            if cross == 0:
                total = merged[color, sub, 0, y].astype(jnp.float32)
            for step in (0, 1, 3, 2):
                slot = step * 2 + cross
                if slot != 0:
                    landing = final.at[color, sub, slot]
                    remote(landing, landing, send_f.at[color, sub, slot], recv_f.at[color, sub, slot], me).wait_recv()
                    total = total + final[color, sub, slot].astype(jnp.float32)
            side = 1 - y if cross else y
            at = pl.multiple_of(side * 4096 + sub * 2048 + color * 1024, 1024)
            out_ref[:, pl.ds(at, 1024)] = total.astype(jnp.bfloat16)

    def arrived(slot):
        there = slab.at[pl.ds(pl.multiple_of((1 - y) * 256, 256), 256), pl.ds(columns[slot][0], columns[slot][1])]
        remote(there, there, send_w.at[slot], recv_w.at[slot], me).wait_recv()

    arrived(0)
    compute(0, 0, 2)
    start_far(0, 0)
    compute(1, 0, 2)
    start_far(1, 0)
    for color in range(2):
        compute(color, 0, 1)
        compute(color, 0, 3)
        start_plain(color, 0)
    for color in range(2):
        compute(color, 0, 0)
    for color in range(2):
        relay(color, 0)
    arrived(1)
    compute(0, 1, 2)
    start_far(0, 1)
    compute(0, 1, 1)
    compute(0, 1, 3)
    start_plain(0, 1)
    compute(0, 1, 0)
    arrived(2)
    compute(1, 1, 2)
    start_far(1, 1)
    compute(1, 1, 1)
    compute(1, 1, 3)
    start_plain(1, 1)
    compute(1, 1, 0)
    for color in range(2):
        second_stage(color, 0)
    for color in range(2):
        relay(color, 1)
    for color in range(2):
        finish(color, 0)
    for color in range(2):
        second_stage(color, 1)
    for color in range(2):
        finish(color, 1)
    for copy in pending:
        copy.wait_send()
    for copy in gathers_z + gathers_x + [gather_y] + rest + over_z + over_x:
        copy.wait_send()
    for step in range(1, 8):
        remote(start.at[spot], start.at[spot], send_0.at[step], recv_0.at[spot], me).wait_send()
    for group in range(4):
        across(group).wait_send()

        @pl.when(group != x)
        def _():
            onward(group).wait_send()


def rotate_and_project(rows, rotations, slab, early):
    bf = jnp.bfloat16
    dma = pltpu.SemaphoreType.DMA
    return pl.pallas_call(
        main_kernel,
        out_shape=jax.ShapeDtypeStruct((32, 8192), bf),
        in_specs=[pl.BlockSpec(memory_space=pltpu.VMEM)] * 2 + [pl.BlockSpec(memory_space=pl.ANY)] * 2,
        out_specs=pl.BlockSpec(memory_space=pltpu.VMEM),
        scratch_shapes=[
            pltpu.VMEM((2, 4, 2, BLK, BLK), bf),
            pltpu.VMEM((2, 4, 2, BLK, BLK), bf),
            pltpu.VMEM((2, 2, 2, BLK, BLK), bf),
            pltpu.VMEM((8, 32, 1024), bf),
            pltpu.VMEM((4, 256, 256), bf),
            pltpu.VMEM((4, 256, 256), bf),
            pltpu.VMEM((4, 256, 256), bf),
            pltpu.VMEM((4, 256, 256), bf),
            pltpu.VMEM((2, 4, 256, 256), bf),
        ]
        + [dma((count,)) for count in (8, 8, 7, 7, 4, 4, 4, 4, 4, 4, 4, 4, 3, 3)]
        + [
            dma,
            pltpu.VMEM((4, 256, 512), bf),
            pltpu.VMEM((512, 4096), bf),
            pltpu.VMEM((2, 2, 4, 2, 256, 512), bf),
            pltpu.VMEM((2, 2, 2, 256, 512), bf),
            pltpu.VMEM((2, 2, 2, 2, 256, 512), bf),
            pltpu.VMEM((2, 2, 4, 2, 32, 1024), bf),
            pltpu.VMEM((2, 2, 8, 32, 1024), bf),
            dma((2, 2, 6)),
            dma((2, 2, 6)),
            dma((2, 2, 8)),
            dma((2, 2, 8)),
            dma,
        ],
        compiler_params=pltpu.CompilerParams(collective_id=1, has_side_effects=True, vmem_limit_bytes=52 * 2**20),
        cost_estimate=pl.CostEstimate(flops=2 * 1024 * 512 * 4096, bytes_accessed=10 * 2**20, transcendentals=0),
    )(rows, rotations, slab, early)


def shards(weight_slab, token_rows, skew_params, pairing):
    side = lax.axis_index("tensor") % 2
    outgoing = lax.dynamic_slice_in_dim(weight_slab, (1 - side) * 4096, 768, 1)
    early = lax.ppermute(outgoing, "tensor", [(d, d ^ 1) for d in range(32)])
    return rotate_and_project(token_rows, cayley_blocks(skew_params, pairing), weight_slab, early)


def solution(mesh):
    in_specs = (
        P(("layer", "tensor"), None),
        P(("layer", "tensor"), None),
        P("layer", "tensor", None, None),
        P("layer", None),
    )
    out_specs = P(("layer", "tensor"), None)
    return jax.shard_map(shards, mesh=mesh, in_specs=in_specs, out_specs=out_specs, check_vma=False)
```

```python
import jax
import jax.numpy as jnp
import numpy as np
from jax import lax
from jax.experimental import pallas as pl
from jax.experimental.pallas import tpu as pltpu
from jax.sharding import PartitionSpec as P

HALF = 64
BLK = 128


def pair_table(distance, count):
    stride = 1 << distance
    rows = []
    for group in range(count // (2 * stride)):
        for offset in range(stride):
            low = group * 2 * stride + offset
            member = low if low >> 1 & 1 == 0 else low + stride
            rows.append((low, low + stride, (member >> 2) * 2 + (member & 1)))
    return rows


def split(value):
    high = value.astype(jnp.bfloat16)
    return high, (value - high.astype(jnp.float32)).astype(jnp.bfloat16)


def as_left(high, low):
    return jnp.concatenate([high, low], axis=1)


def as_right(high, low):
    row = jnp.concatenate([high, low], axis=1)
    return jnp.concatenate([row, row], axis=0)


def wide_dot(left, right):
    return jnp.dot(left, right, preferred_element_type=jnp.float32)


def folded_dot(left, right):
    both = wide_dot(left, right)
    return both[:, :BLK] + both[:, BLK:]


def split_three(value):
    high = value.astype(jnp.bfloat16)
    left_over = value - high.astype(jnp.float32)
    middle = left_over.astype(jnp.bfloat16)
    return high, middle, (left_over - middle.astype(jnp.float32)).astype(jnp.bfloat16)


def full_dot(left, right):
    left_hi, left_mid, left_lo = split_three(left)
    right_hi, right_mid, right_lo = split_three(right)
    small = wide_dot(as_left(left_hi, left_lo), jnp.concatenate([right_lo, right_hi], axis=0))
    return folded_dot(as_left(left_hi, left_mid), as_right(right_hi, right_mid)) + small


def rotation_kernel(skew_ref, pairing_ref, out_ref, gram, gram_left, guess):
    count = gram.shape[0]
    rows = lax.broadcasted_iota(jnp.int32, (BLK, BLK), 0)
    lanes = lax.broadcasted_iota(jnp.int32, (BLK, BLK), 1)
    identity = (rows == lanes).astype(jnp.float32)
    largest = jnp.zeros((1, 1), jnp.float32)
    for block in range(count):
        raw = skew_ref[block]
        skewed = raw - raw.T
        square = full_dot(skewed, skewed)
        shifted = identity - square
        gram[block] = shifted
        gram_left[block] = as_left(*split(shifted))
        rounded = square.astype(jnp.bfloat16)
        fourth = jnp.dot(rounded, rounded, preferred_element_type=jnp.float32)
        largest = jnp.maximum(largest, jnp.sum(jnp.sum(fourth * fourth, axis=0, keepdims=True), axis=1, keepdims=True))
    top = 1.0 + 1.02 * jnp.sqrt(jnp.sqrt(0.5 * jnp.max(largest)))
    start = 2.0 / (1.0 + top)
    for block in range(count):
        guess[block] = identity * start

    def more(state):
        return state > 1e-2

    def improve(spread):
        shrunk = spread * spread / (2.0 - spread * spread)
        scale = 2.0 / (2.0 - spread * spread)
        for block in range(count):
            high, low = split(guess[block])
            left = 2.0 * identity - folded_dot(gram_left[block], as_right(high, low))
            guess[block] = scale * folded_dot(as_left(high, low), as_right(*split(left)))
        return shrunk

    lax.while_loop(more, improve, (top - 1.0) / (top + 1.0))
    for section in range(count // 2):
        turned = []
        for block in (2 * section, 2 * section + 1):
            raw = skew_ref[block]
            raised = identity + raw - raw.T
            now = guess[block]
            miss = identity - full_dot(gram[block], now)
            now = now + folded_dot(as_left(*split(now)), as_right(*split(miss)))
            rotation = 2.0 * folded_dot(as_left(*split(now)), as_right(*split(raised))) - identity
            turned.append(rotation.astype(jnp.bfloat16))
        order = pairing_ref[pl.ds(section, 1), :]
        chosen = (rows == order).astype(jnp.float32)
        inner = wide_dot(chosen.astype(jnp.bfloat16), jnp.concatenate(turned, axis=1)).astype(jnp.bfloat16)
        stacked = jnp.concatenate([inner[:, :BLK], inner[:, BLK:]], axis=0)
        outer = wide_dot(stacked, chosen.T.astype(jnp.bfloat16)).astype(jnp.bfloat16)
        out_ref[2 * section] = outer[:BLK]
        out_ref[2 * section + 1] = outer[BLK:]


def cayley_blocks(skew_params, pairing):
    sections, owned = skew_params.shape[:2]
    count = sections * owned
    out = pl.pallas_call(
        rotation_kernel,
        out_shape=jax.ShapeDtypeStruct((count, BLK, BLK), jnp.bfloat16),
        in_specs=[pl.BlockSpec(memory_space=pltpu.VMEM)] * 2,
        out_specs=pl.BlockSpec(memory_space=pltpu.VMEM),
        scratch_shapes=[
            pltpu.VMEM((count, BLK, BLK), jnp.float32),
            pltpu.VMEM((count, BLK, 2 * BLK), jnp.bfloat16),
            pltpu.VMEM((count, BLK, BLK), jnp.float32),
        ],
        compiler_params=pltpu.CompilerParams(vmem_limit_bytes=16 * 2**20),
        cost_estimate=pl.CostEstimate(flops=count * BLK**3 * 20, bytes_accessed=count * BLK * BLK * 6, transcendentals=0),
    )(skew_params.reshape(count, BLK, BLK), pairing)
    return out.reshape(sections, owned, BLK, BLK)


def halves_dot(value, rotation_of, distance):
    halves = value.shape[1] // HALF
    parts = [None] * halves
    for low, high, owner in pair_table(distance, halves):
        joined = jnp.concatenate([value[:, low * HALF:(low + 1) * HALF], value[:, high * HALF:(high + 1) * HALF]], axis=1)
        turned = jnp.dot(joined, rotation_of(owner), preferred_element_type=jnp.float32).astype(jnp.bfloat16)
        parts[low], parts[high] = turned[:, :HALF], turned[:, HALF:]
    return jnp.concatenate(parts, axis=1)


def place():
    me = lax.axis_index("tensor")
    return me, me // 8, (me // 2) % 4, me % 2


def remote(src, dst, send, recv, peer):
    return pltpu.make_async_remote_copy(
        src_ref=src, dst_ref=dst, send_sem=send, recv_sem=recv,
        device_id={"tensor": peer}, device_id_type=pl.DeviceIdType.MESH,
    )


def greet(peers):
    barrier = pltpu.get_barrier_semaphore()
    for peer in peers:
        pl.semaphore_signal(barrier, inc=1, device_id={"tensor": peer}, device_id_type=pl.DeviceIdType.MESH)
    pl.semaphore_wait(barrier, len(peers))


def main_kernel(rows_ref, rot_ref, slab_ref, early_ref, out_ref, rot_z, rot_x, rot_y, start, first, mid, second, third, landed, send_0, recv_0, send_e, recv_e, send_1, recv_1, send_2, recv_2, send_3, recv_3, send_4, recv_4, send_w, recv_w, own_w, tokens, slab, part, far, near, merged, final, send, recv, send_f, recv_f, early_w):
    me, z, x, y = place()
    spot = x * 2 + y
    own = pltpu.make_async_copy(slab_ref.at[:, pl.ds(pl.multiple_of(y * 4096, 4096), 4096)], slab.at[pl.ds(pl.multiple_of(y * 256, 256), 256)], own_w)
    own.start()
    early = pltpu.make_async_copy(early_ref, slab.at[pl.ds(pl.multiple_of((1 - y) * 256, 256), 256), pl.ds(0, 1024)], early_w)
    early.start()
    partner = z * 8 + x * 2 + 1 - y
    greet([((z + step) % 4) * 8 + spot for step in range(1, 4)] + [z * 8 + (spot + step) % 8 for step in range(1, 8)] + [((z + step) % 4) * 8 + x * 2 + 1 - y for step in range(1, 4)])

    def gather(slot, source, target, peer):
        return remote(source, target, send_e.at[slot], recv_e.at[slot], peer)

    gathers_z = [gather(step - 1, rot_ref.at[pl.ds(4, 2)], rot_z.at[:, z], ((z + step) % 4) * 8 + spot) for step in (1, 3, 2)]
    gathers_x = [gather(2 + step, rot_ref.at[pl.ds(2, 2)], rot_x.at[:, x], z * 8 + ((x + step) % 4) * 2 + y) for step in (1, 3, 2)]
    gather_y = gather(6, rot_ref.at[pl.ds(0, 2)], rot_y.at[:, y], z * 8 + x * 2 + 1 - y)
    for copy in gathers_z:
        copy.start()

    def piece_of(other, group):
        at = pl.multiple_of(group * 2048 + other * 256, 256)
        return rows_ref.at[:, pl.ds(at, 256)]

    for step in range(1, 8):
        other = (spot + step) % 8
        for group in range(4):
            remote(piece_of(other, group), start.at[spot, :, pl.ds(group * 256, 256)], send_0.at[step], recv_0.at[spot], z * 8 + other).start()
    gather_y.start()

    columns = [(1024, 1024), (2048, 1024), (3072, 1024)]
    rest = []
    for slot, (first_col, width) in enumerate(columns):
        source = slab_ref.at[:, pl.ds(pl.multiple_of((1 - y) * 4096 + first_col, 256), width)]
        target = slab.at[pl.ds(pl.multiple_of(y * 256, 256), 256), pl.ds(first_col, width)]
        rest.append(remote(source, target, send_w.at[slot], recv_w.at[slot], partner))
    rest[0].start()
    for group in range(4):
        start[spot, :, group * 256:(group + 1) * 256] = rows_ref[:, pl.ds(pl.multiple_of(group * 2048 + spot * 256, 256), 256)]
    rot_z[:, z] = rot_ref[4:6]
    rot_x[:, x] = rot_ref[2:4]
    rot_y[:, y] = rot_ref[0:2]
    for step in range(1, 8):
        other = (spot + step) % 8
        remote(start.at[spot], start.at[other], send_0.at[step], recv_0.at[other], me).wait_recv()
    for copy in gathers_z:
        copy.wait_recv()
    for copy in gathers_x:
        copy.start()
    value = jnp.concatenate([start[other] for other in range(8)], axis=0)
    value = halves_dot(value, lambda k: rot_z[1, k // 2, k % 2], 3)
    value = halves_dot(value, lambda k: rot_z[0, k // 2, k % 2], 2)
    for piece in range(4):
        first[piece] = value[:, piece * 256:(piece + 1) * 256]

    over_z = [remote(first.at[(z + step) % 4], mid.at[z], send_1.at[step], recv_1.at[z], ((z + step) % 4) * 8 + spot) for step in (1, 3, 2)]
    for copy in over_z:
        copy.start()
    mid[z] = first[z]

    def onward(group):
        return remote(mid.at[group], second.at[x], send_2.at[group], recv_2.at[x], z * 8 + group * 2 + y)

    for step in (0, 3, 1, 2):
        group = (z + step) % 4
        if step != 0:
            remote(first.at[0], mid.at[group], send_1.at[step], recv_1.at[group], me).wait_recv()

        @pl.when(group != x)
        def _():
            onward(group).start()

        @pl.when(group == x)
        def _():
            second[x] = mid[group]

    for step in (1, 3, 2):
        source = (x + step) % 4
        remote(mid.at[0], second.at[source], send_2.at[0], recv_2.at[source], me).wait_recv()
    for copy in gathers_x:
        copy.wait_recv()
    value = jnp.concatenate([second[piece] for piece in range(4)], axis=1)
    value = halves_dot(value, lambda k: rot_x[1, k // 2, k % 2], 3)
    value = halves_dot(value, lambda k: rot_x[0, k // 2, k % 2], 2)
    for piece in range(4):
        third[piece] = value[:, piece * 256:(piece + 1) * 256]

    over_x = [remote(third.at[(x + step) % 4], landed.at[y, x], send_3.at[step], recv_3.at[x], z * 8 + ((x + step) % 4) * 2 + y) for step in (1, 3, 2)]
    for copy in over_x:
        copy.start()
    landed[y, x] = third[x]

    def across(group):
        return remote(landed.at[y, group], landed.at[y, group], send_4.at[group], recv_4.at[group], z * 8 + x * 2 + 1 - y)

    for step in (0, 3, 1, 2):
        group = (x + step) % 4
        if step != 0:
            remote(third.at[0], landed.at[y, group], send_3.at[step], recv_3.at[group], me).wait_recv()
        across(group).start()
    for copy in rest[1:]:
        copy.start()
    gather_y.wait_recv()
    for step in (0, 3, 1, 2):
        group = (x + step) % 4
        remote(landed.at[y, group], landed.at[1 - y, group], send_4.at[group], recv_4.at[group], me).wait_recv()
        value = jnp.concatenate([landed[0, group], landed[1, group]], axis=1)
        value = halves_dot(value, lambda k: rot_y[1, k // 2, k % 2], 2)
        value = halves_dot(value, lambda k: rot_y[0, k // 2, k % 2], 0)
        tokens[group] = value
    own.wait()
    early.wait()

    coords = (z, x)

    def peer(axis, step):
        if axis == 0:
            return ((z + step) % 4) * 8 + spot
        return z * 8 + ((x + step) % 4) * 2 + y

    def compute(color, sub, role):
        block = (coords[color] + role) % 4
        if color == 0:
            left = tokens[block]
        else:
            left = jnp.concatenate([tokens[group, pl.ds(pl.multiple_of(block * 64, 64), 64), :] for group in range(4)], axis=0)

        def tile(half, carry):
            at = pl.multiple_of(sub * 2048 + color * 1024 + half * 512, 512)
            part[color, sub, role, half] = jnp.dot(left, slab[:, pl.ds(at, 512)], preferred_element_type=jnp.float32).astype(jnp.bfloat16)
            return carry

        lax.fori_loop(0, 2, tile, 0)

    pending = []

    def ship(color, sub, slot, source, target, step):
        copy = remote(source, target, send.at[color, sub, slot], recv.at[color, sub, slot], peer(color, step))
        copy.start()
        pending.append(copy)
        return copy

    fars, nears = {}, {}

    def start_far(color, sub):
        fars[color, sub] = (
            ship(color, sub, 0, part.at[color, sub, 2, 0], far.at[color, sub, 0], 1),
            ship(color, sub, 1, part.at[color, sub, 2, 1], far.at[color, sub, 1], 3),
        )

    def start_plain(color, sub):
        nears[color, sub] = [
            ship(color, sub, 2, part.at[color, sub, 1, 1], near.at[color, sub, 0, 1], 1),
            ship(color, sub, 3, part.at[color, sub, 3, 0], near.at[color, sub, 1, 0], 3),
        ]

    def add(a, b):
        return (a.astype(jnp.float32) + b.astype(jnp.float32)).astype(jnp.bfloat16)

    def relay(color, sub):
        fars[color, sub][0].wait_recv()
        part[color, sub, 1, 0] = add(part[color, sub, 1, 0], far[color, sub, 0])
        up = ship(color, sub, 4, part.at[color, sub, 1, 0], near.at[color, sub, 0, 0], 1)
        fars[color, sub][1].wait_recv()
        part[color, sub, 3, 1] = add(part[color, sub, 3, 1], far[color, sub, 1])
        down = ship(color, sub, 5, part.at[color, sub, 3, 1], near.at[color, sub, 1, 1], 3)
        nears[color, sub] += [up, down]

    def owner(color, step, cross):
        side = 1 - y if cross else y
        if color == 0:
            return z * 8 + ((x + step) % 4) * 2 + side
        return ((z + step) % 4) * 8 + x * 2 + side

    def second_stage(color, sub):
        for copy in nears[color, sub]:
            copy.wait_recv()
        here = coords[1 - color]
        for step in (2, 1, 3, 0):
            there = (here + step) % 4
            at = pl.ds(pl.multiple_of(there * 64, 64), 64)
            for half in range(2):
                total = part[color, sub, 0, half, at, :].astype(jnp.float32)
                total = total + near[color, sub, 0, half, at, :].astype(jnp.float32) + near[color, sub, 1, half, at, :].astype(jnp.float32)
                total = total.astype(jnp.bfloat16)
                merged[color, sub, step, 0, :, half * 512:half * 512 + 512] = total[:32]
                merged[color, sub, step, 1, :, half * 512:half * 512 + 512] = total[32:]
            for cross in (1, 0):
                if step != 0 or cross == 1:
                    side = 1 - y if cross else y
                    slot = step * 2 + cross
                    copy = remote(merged.at[color, sub, step, side], final.at[color, sub, slot], send_f.at[color, sub, slot], recv_f.at[color, sub, slot], owner(color, step, cross))
                    copy.start()
                    pending.append(copy)

    def finish(color, sub):
        for cross in (0, 1):
            total = jnp.zeros((32, 1024), jnp.float32)
            if cross == 0:
                total = merged[color, sub, 0, y].astype(jnp.float32)
            for step in (0, 1, 3, 2):
                slot = step * 2 + cross
                if slot != 0:
                    landing = final.at[color, sub, slot]
                    remote(landing, landing, send_f.at[color, sub, slot], recv_f.at[color, sub, slot], me).wait_recv()
                    total = total + final[color, sub, slot].astype(jnp.float32)
            side = 1 - y if cross else y
            at = pl.multiple_of(side * 4096 + sub * 2048 + color * 1024, 1024)
            out_ref[:, pl.ds(at, 1024)] = total.astype(jnp.bfloat16)

    def arrived(slot):
        there = slab.at[pl.ds(pl.multiple_of((1 - y) * 256, 256), 256), pl.ds(columns[slot][0], columns[slot][1])]
        remote(there, there, send_w.at[slot], recv_w.at[slot], me).wait_recv()

    compute(0, 0, 2)
    start_far(0, 0)
    arrived(0)
    compute(1, 0, 2)
    start_far(1, 0)
    for color in range(2):
        compute(color, 0, 1)
        compute(color, 0, 3)
        start_plain(color, 0)
    for color in range(2):
        compute(color, 0, 0)
    for color in range(2):
        relay(color, 0)
    arrived(1)
    compute(0, 1, 2)
    start_far(0, 1)
    compute(0, 1, 1)
    compute(0, 1, 3)
    start_plain(0, 1)
    compute(0, 1, 0)
    arrived(2)
    compute(1, 1, 2)
    start_far(1, 1)
    compute(1, 1, 1)
    compute(1, 1, 3)
    start_plain(1, 1)
    compute(1, 1, 0)
    for color in range(2):
        relay(color, 1)
    for sub in range(2):
        for color in range(2):
            second_stage(color, sub)
    for sub in range(2):
        for color in range(2):
            finish(color, sub)
    for copy in pending:
        copy.wait_send()
    for copy in gathers_z + gathers_x + [gather_y] + rest + over_z + over_x:
        copy.wait_send()
    for step in range(1, 8):
        remote(start.at[spot], start.at[spot], send_0.at[step], recv_0.at[spot], me).wait_send()
    for group in range(4):
        across(group).wait_send()

        @pl.when(group != x)
        def _():
            onward(group).wait_send()


def rotate_and_project(rows, rotations, slab, early):
    bf = jnp.bfloat16
    dma = pltpu.SemaphoreType.DMA
    return pl.pallas_call(
        main_kernel,
        out_shape=jax.ShapeDtypeStruct((32, 8192), bf),
        in_specs=[pl.BlockSpec(memory_space=pltpu.VMEM)] * 2 + [pl.BlockSpec(memory_space=pl.ANY)] * 2,
        out_specs=pl.BlockSpec(memory_space=pltpu.VMEM),
        scratch_shapes=[
            pltpu.VMEM((2, 4, 2, BLK, BLK), bf),
            pltpu.VMEM((2, 4, 2, BLK, BLK), bf),
            pltpu.VMEM((2, 2, 2, BLK, BLK), bf),
            pltpu.VMEM((8, 32, 1024), bf),
            pltpu.VMEM((4, 256, 256), bf),
            pltpu.VMEM((4, 256, 256), bf),
            pltpu.VMEM((4, 256, 256), bf),
            pltpu.VMEM((4, 256, 256), bf),
            pltpu.VMEM((2, 4, 256, 256), bf),
        ]
        + [dma((count,)) for count in (8, 8, 7, 7, 4, 4, 4, 4, 4, 4, 4, 4, 3, 3)]
        + [
            dma,
            pltpu.VMEM((4, 256, 512), bf),
            pltpu.VMEM((512, 4096), bf),
            pltpu.VMEM((2, 2, 4, 2, 256, 512), bf),
            pltpu.VMEM((2, 2, 2, 256, 512), bf),
            pltpu.VMEM((2, 2, 2, 2, 256, 512), bf),
            pltpu.VMEM((2, 2, 4, 2, 32, 1024), bf),
            pltpu.VMEM((2, 2, 8, 32, 1024), bf),
            dma((2, 2, 6)),
            dma((2, 2, 6)),
            dma((2, 2, 8)),
            dma((2, 2, 8)),
            dma,
        ],
        compiler_params=pltpu.CompilerParams(collective_id=1, has_side_effects=True, vmem_limit_bytes=52 * 2**20),
        cost_estimate=pl.CostEstimate(flops=2 * 1024 * 512 * 4096, bytes_accessed=10 * 2**20, transcendentals=0),
    )(rows, rotations, slab, early)


def shards(weight_slab, token_rows, skew_params, pairing):
    side = lax.axis_index("tensor") % 2
    outgoing = lax.dynamic_slice_in_dim(weight_slab, (1 - side) * 4096, 1024, 1)
    early = lax.ppermute(outgoing, "tensor", [(d, d ^ 1) for d in range(32)])
    return rotate_and_project(token_rows, cayley_blocks(skew_params, pairing), weight_slab, early)


def solution(mesh):
    in_specs = (
        P(("layer", "tensor"), None),
        P(("layer", "tensor"), None),
        P("layer", "tensor", None, None),
        P("layer", None),
    )
    out_specs = P(("layer", "tensor"), None)
    return jax.shard_map(shards, mesh=mesh, in_specs=in_specs, out_specs=out_specs, check_vma=False)
```

```python
import jax
import jax.numpy as jnp
import numpy as np
from jax import lax
from jax.experimental import pallas as pl
from jax.experimental.pallas import tpu as pltpu
from jax.sharding import PartitionSpec as P

HALF = 64
BLK = 128


def pair_table(distance, count):
    stride = 1 << distance
    rows = []
    for group in range(count // (2 * stride)):
        for offset in range(stride):
            low = group * 2 * stride + offset
            member = low if low >> 1 & 1 == 0 else low + stride
            rows.append((low, low + stride, (member >> 2) * 2 + (member & 1)))
    return rows


def split(value):
    high = value.astype(jnp.bfloat16)
    return high, (value - high.astype(jnp.float32)).astype(jnp.bfloat16)


def as_left(high, low):
    return jnp.concatenate([high, low], axis=1)


def as_right(high, low):
    row = jnp.concatenate([high, low], axis=1)
    return jnp.concatenate([row, row], axis=0)


def wide_dot(left, right):
    return jnp.dot(left, right, preferred_element_type=jnp.float32)


def folded_dot(left, right):
    both = wide_dot(left, right)
    return both[:, :BLK] + both[:, BLK:]


def split_three(value):
    high = value.astype(jnp.bfloat16)
    left_over = value - high.astype(jnp.float32)
    middle = left_over.astype(jnp.bfloat16)
    return high, middle, (left_over - middle.astype(jnp.float32)).astype(jnp.bfloat16)


def full_dot(left, right):
    left_hi, left_mid, left_lo = split_three(left)
    right_hi, right_mid, right_lo = split_three(right)
    small = wide_dot(as_left(left_hi, left_lo), jnp.concatenate([right_lo, right_hi], axis=0))
    return folded_dot(as_left(left_hi, left_mid), as_right(right_hi, right_mid)) + small


def rotation_kernel(skew_ref, pairing_ref, out_ref, gram, gram_left, guess):
    count = gram.shape[0]
    rows = lax.broadcasted_iota(jnp.int32, (BLK, BLK), 0)
    lanes = lax.broadcasted_iota(jnp.int32, (BLK, BLK), 1)
    identity = (rows == lanes).astype(jnp.float32)
    largest = jnp.zeros((1, 1), jnp.float32)
    for block in range(count):
        raw = skew_ref[block]
        skewed = raw - raw.T
        square = full_dot(skewed, skewed)
        shifted = identity - square
        gram[block] = shifted
        gram_left[block] = as_left(*split(shifted))
        rounded = square.astype(jnp.bfloat16)
        fourth = jnp.dot(rounded, rounded, preferred_element_type=jnp.float32)
        largest = jnp.maximum(largest, jnp.sum(jnp.sum(fourth * fourth, axis=0, keepdims=True), axis=1, keepdims=True))
    top = 1.0 + 1.02 * jnp.sqrt(jnp.sqrt(0.5 * jnp.max(largest)))
    start = 2.0 / (1.0 + top)
    for block in range(count):
        guess[block] = identity * start

    def more(state):
        return state > 1e-2

    def improve(spread):
        shrunk = spread * spread / (2.0 - spread * spread)
        scale = 2.0 / (2.0 - spread * spread)
        for block in range(count):
            high, low = split(guess[block])
            left = 2.0 * identity - folded_dot(gram_left[block], as_right(high, low))
            guess[block] = scale * folded_dot(as_left(high, low), as_right(*split(left)))
        return shrunk

    lax.while_loop(more, improve, (top - 1.0) / (top + 1.0))
    for section in range(count // 2):
        turned = []
        for block in (2 * section, 2 * section + 1):
            raw = skew_ref[block]
            raised = identity + raw - raw.T
            now = guess[block]
            miss = identity - full_dot(gram[block], now)
            now = now + folded_dot(as_left(*split(now)), as_right(*split(miss)))
            rotation = 2.0 * folded_dot(as_left(*split(now)), as_right(*split(raised))) - identity
            turned.append(rotation.astype(jnp.bfloat16))
        order = pairing_ref[pl.ds(section, 1), :]
        chosen = (rows == order).astype(jnp.float32)
        inner = wide_dot(chosen.astype(jnp.bfloat16), jnp.concatenate(turned, axis=1)).astype(jnp.bfloat16)
        stacked = jnp.concatenate([inner[:, :BLK], inner[:, BLK:]], axis=0)
        outer = wide_dot(stacked, chosen.T.astype(jnp.bfloat16)).astype(jnp.bfloat16)
        out_ref[2 * section] = outer[:BLK]
        out_ref[2 * section + 1] = outer[BLK:]


def cayley_blocks(skew_params, pairing):
    sections, owned = skew_params.shape[:2]
    count = sections * owned
    out = pl.pallas_call(
        rotation_kernel,
        out_shape=jax.ShapeDtypeStruct((count, BLK, BLK), jnp.bfloat16),
        in_specs=[pl.BlockSpec(memory_space=pltpu.VMEM)] * 2,
        out_specs=pl.BlockSpec(memory_space=pltpu.VMEM),
        scratch_shapes=[
            pltpu.VMEM((count, BLK, BLK), jnp.float32),
            pltpu.VMEM((count, BLK, 2 * BLK), jnp.bfloat16),
            pltpu.VMEM((count, BLK, BLK), jnp.float32),
        ],
        compiler_params=pltpu.CompilerParams(vmem_limit_bytes=16 * 2**20),
        cost_estimate=pl.CostEstimate(flops=count * BLK**3 * 20, bytes_accessed=count * BLK * BLK * 6, transcendentals=0),
    )(skew_params.reshape(count, BLK, BLK), pairing)
    return out.reshape(sections, owned, BLK, BLK)


def halves_dot(value, rotation_of, distance):
    halves = value.shape[1] // HALF
    parts = [None] * halves
    for low, high, owner in pair_table(distance, halves):
        joined = jnp.concatenate([value[:, low * HALF:(low + 1) * HALF], value[:, high * HALF:(high + 1) * HALF]], axis=1)
        turned = jnp.dot(joined, rotation_of(owner), preferred_element_type=jnp.float32).astype(jnp.bfloat16)
        parts[low], parts[high] = turned[:, :HALF], turned[:, HALF:]
    return jnp.concatenate(parts, axis=1)


def place():
    me = lax.axis_index("tensor")
    return me, me // 8, (me // 2) % 4, me % 2


def remote(src, dst, send, recv, peer):
    return pltpu.make_async_remote_copy(
        src_ref=src, dst_ref=dst, send_sem=send, recv_sem=recv,
        device_id={"tensor": peer}, device_id_type=pl.DeviceIdType.MESH,
    )


def greet(peers):
    barrier = pltpu.get_barrier_semaphore()
    for peer in peers:
        pl.semaphore_signal(barrier, inc=1, device_id={"tensor": peer}, device_id_type=pl.DeviceIdType.MESH)
    pl.semaphore_wait(barrier, len(peers))


def main_kernel(rows_ref, rot_ref, slab_ref, early_ref, out_ref, rot_z, rot_x, rot_y, start, first, mid, second, third, landed, send_0, recv_0, send_e, recv_e, send_1, recv_1, send_2, recv_2, send_3, recv_3, send_4, recv_4, send_w, recv_w, own_w, tokens, slab, part, far, near, merged, final, send, recv, send_f, recv_f, early_w):
    me, z, x, y = place()
    spot = x * 2 + y
    own = pltpu.make_async_copy(slab_ref.at[:, pl.ds(pl.multiple_of(y * 4096, 4096), 4096)], slab.at[pl.ds(pl.multiple_of(y * 256, 256), 256)], own_w)
    own.start()
    early = pltpu.make_async_copy(early_ref, slab.at[pl.ds(pl.multiple_of((1 - y) * 256, 256), 256), pl.ds(0, 1024)], early_w)
    early.start()
    partner = z * 8 + x * 2 + 1 - y
    greet([((z + step) % 4) * 8 + spot for step in range(1, 4)] + [z * 8 + (spot + step) % 8 for step in range(1, 8)] + [((z + step) % 4) * 8 + x * 2 + 1 - y for step in range(1, 4)])

    def gather(slot, source, target, peer):
        return remote(source, target, send_e.at[slot], recv_e.at[slot], peer)

    gathers_z = [gather(step - 1, rot_ref.at[pl.ds(4, 2)], rot_z.at[:, z], ((z + step) % 4) * 8 + spot) for step in (1, 3, 2)]
    gathers_x = [gather(2 + step, rot_ref.at[pl.ds(2, 2)], rot_x.at[:, x], z * 8 + ((x + step) % 4) * 2 + y) for step in (1, 3, 2)]
    gather_y = gather(6, rot_ref.at[pl.ds(0, 2)], rot_y.at[:, y], z * 8 + x * 2 + 1 - y)
    for copy in gathers_z:
        copy.start()

    def piece_of(other, group):
        at = pl.multiple_of(group * 2048 + other * 256, 256)
        return rows_ref.at[:, pl.ds(at, 256)]

    for step in range(1, 8):
        other = (spot + step) % 8
        for group in range(4):
            remote(piece_of(other, group), start.at[spot, :, pl.ds(group * 256, 256)], send_0.at[step], recv_0.at[spot], z * 8 + other).start()
    for copy in gathers_x + [gather_y]:
        copy.start()

    columns = [(1024, 1024), (2048, 1024), (3072, 1024)]
    rest = []
    for slot, (first_col, width) in enumerate(columns):
        source = slab_ref.at[:, pl.ds(pl.multiple_of((1 - y) * 4096 + first_col, 256), width)]
        target = slab.at[pl.ds(pl.multiple_of(y * 256, 256), 256), pl.ds(first_col, width)]
        rest.append(remote(source, target, send_w.at[slot], recv_w.at[slot], partner))
    rest[0].start()
    for group in range(4):
        start[spot, :, group * 256:(group + 1) * 256] = rows_ref[:, pl.ds(pl.multiple_of(group * 2048 + spot * 256, 256), 256)]
    rot_z[:, z] = rot_ref[4:6]
    rot_x[:, x] = rot_ref[2:4]
    rot_y[:, y] = rot_ref[0:2]
    for step in range(1, 8):
        other = (spot + step) % 8
        remote(start.at[spot], start.at[other], send_0.at[step], recv_0.at[other], me).wait_recv()
    for copy in gathers_z:
        copy.wait_recv()
    value = jnp.concatenate([start[other] for other in range(8)], axis=0)
    value = halves_dot(value, lambda k: rot_z[1, k // 2, k % 2], 3)
    value = halves_dot(value, lambda k: rot_z[0, k // 2, k % 2], 2)
    for piece in range(4):
        first[piece] = value[:, piece * 256:(piece + 1) * 256]

    over_z = [remote(first.at[(z + step) % 4], mid.at[z], send_1.at[step], recv_1.at[z], ((z + step) % 4) * 8 + spot) for step in (1, 3, 2)]
    for copy in over_z:
        copy.start()
    mid[z] = first[z]

    def onward(group):
        return remote(mid.at[group], second.at[x], send_2.at[group], recv_2.at[x], z * 8 + group * 2 + y)

    for step in (0, 3, 1, 2):
        group = (z + step) % 4
        if step != 0:
            remote(first.at[0], mid.at[group], send_1.at[step], recv_1.at[group], me).wait_recv()

        @pl.when(group != x)
        def _():
            onward(group).start()

        @pl.when(group == x)
        def _():
            second[x] = mid[group]

    for step in (1, 3, 2):
        source = (x + step) % 4
        remote(mid.at[0], second.at[source], send_2.at[0], recv_2.at[source], me).wait_recv()
    for copy in gathers_x:
        copy.wait_recv()
    value = jnp.concatenate([second[piece] for piece in range(4)], axis=1)
    value = halves_dot(value, lambda k: rot_x[1, k // 2, k % 2], 3)
    value = halves_dot(value, lambda k: rot_x[0, k // 2, k % 2], 2)
    for piece in range(4):
        third[piece] = value[:, piece * 256:(piece + 1) * 256]

    over_x = [remote(third.at[(x + step) % 4], landed.at[y, x], send_3.at[step], recv_3.at[x], z * 8 + ((x + step) % 4) * 2 + y) for step in (1, 3, 2)]
    for copy in over_x:
        copy.start()
    landed[y, x] = third[x]

    def across(group):
        return remote(landed.at[y, group], landed.at[y, group], send_4.at[group], recv_4.at[group], z * 8 + x * 2 + 1 - y)

    for step in (0, 3, 1, 2):
        group = (x + step) % 4
        if step != 0:
            remote(third.at[0], landed.at[y, group], send_3.at[step], recv_3.at[group], me).wait_recv()
        across(group).start()
    for copy in rest[1:]:
        copy.start()
    gather_y.wait_recv()
    for step in (0, 3, 1, 2):
        group = (x + step) % 4
        remote(landed.at[y, group], landed.at[1 - y, group], send_4.at[group], recv_4.at[group], me).wait_recv()
        value = jnp.concatenate([landed[0, group], landed[1, group]], axis=1)
        value = halves_dot(value, lambda k: rot_y[1, k // 2, k % 2], 2)
        value = halves_dot(value, lambda k: rot_y[0, k // 2, k % 2], 0)
        tokens[group] = value
    own.wait()
    early.wait()

    coords = (z, x)

    def peer(axis, step):
        if axis == 0:
            return ((z + step) % 4) * 8 + spot
        return z * 8 + ((x + step) % 4) * 2 + y

    def compute(color, sub, role):
        block = (coords[color] + role) % 4
        if color == 0:
            left = tokens[block]
        else:
            left = jnp.concatenate([tokens[group, pl.ds(pl.multiple_of(block * 64, 64), 64), :] for group in range(4)], axis=0)

        def tile(half, carry):
            at = pl.multiple_of(sub * 2048 + color * 1024 + half * 512, 512)
            part[color, sub, role, half] = jnp.dot(left, slab[:, pl.ds(at, 512)], preferred_element_type=jnp.float32).astype(jnp.bfloat16)
            return carry

        lax.fori_loop(0, 2, tile, 0)

    pending = []

    def ship(color, sub, slot, source, target, step):
        copy = remote(source, target, send.at[color, sub, slot], recv.at[color, sub, slot], peer(color, step))
        copy.start()
        pending.append(copy)
        return copy

    fars, nears = {}, {}

    def start_far(color, sub):
        fars[color, sub] = (
            ship(color, sub, 0, part.at[color, sub, 2, 0], far.at[color, sub, 0], 1),
            ship(color, sub, 1, part.at[color, sub, 2, 1], far.at[color, sub, 1], 3),
        )

    def start_plain(color, sub):
        nears[color, sub] = [
            ship(color, sub, 2, part.at[color, sub, 1, 1], near.at[color, sub, 0, 1], 1),
            ship(color, sub, 3, part.at[color, sub, 3, 0], near.at[color, sub, 1, 0], 3),
        ]

    def add(a, b):
        return (a.astype(jnp.float32) + b.astype(jnp.float32)).astype(jnp.bfloat16)

    def relay(color, sub):
        fars[color, sub][0].wait_recv()
        part[color, sub, 1, 0] = add(part[color, sub, 1, 0], far[color, sub, 0])
        up = ship(color, sub, 4, part.at[color, sub, 1, 0], near.at[color, sub, 0, 0], 1)
        fars[color, sub][1].wait_recv()
        part[color, sub, 3, 1] = add(part[color, sub, 3, 1], far[color, sub, 1])
        down = ship(color, sub, 5, part.at[color, sub, 3, 1], near.at[color, sub, 1, 1], 3)
        nears[color, sub] += [up, down]

    def owner(color, step, cross):
        side = 1 - y if cross else y
        if color == 0:
            return z * 8 + ((x + step) % 4) * 2 + side
        return ((z + step) % 4) * 8 + x * 2 + side

    def second_stage(color, sub):
        for copy in nears[color, sub]:
            copy.wait_recv()
        here = coords[1 - color]
        for step in (2, 1, 3, 0):
            there = (here + step) % 4
            at = pl.ds(pl.multiple_of(there * 64, 64), 64)
            for half in range(2):
                total = part[color, sub, 0, half, at, :].astype(jnp.float32)
                total = total + near[color, sub, 0, half, at, :].astype(jnp.float32) + near[color, sub, 1, half, at, :].astype(jnp.float32)
                total = total.astype(jnp.bfloat16)
                merged[color, sub, step, 0, :, half * 512:half * 512 + 512] = total[:32]
                merged[color, sub, step, 1, :, half * 512:half * 512 + 512] = total[32:]
            for cross in (1, 0):
                if step != 0 or cross == 1:
                    side = 1 - y if cross else y
                    slot = step * 2 + cross
                    copy = remote(merged.at[color, sub, step, side], final.at[color, sub, slot], send_f.at[color, sub, slot], recv_f.at[color, sub, slot], owner(color, step, cross))
                    copy.start()
                    pending.append(copy)

    def finish(color, sub):
        for cross in (0, 1):
            total = jnp.zeros((32, 1024), jnp.float32)
            if cross == 0:
                total = merged[color, sub, 0, y].astype(jnp.float32)
            for step in (0, 1, 3, 2):
                slot = step * 2 + cross
                if slot != 0:
                    landing = final.at[color, sub, slot]
                    remote(landing, landing, send_f.at[color, sub, slot], recv_f.at[color, sub, slot], me).wait_recv()
                    total = total + final[color, sub, slot].astype(jnp.float32)
            side = 1 - y if cross else y
            at = pl.multiple_of(side * 4096 + sub * 2048 + color * 1024, 1024)
            out_ref[:, pl.ds(at, 1024)] = total.astype(jnp.bfloat16)

    def arrived(slot):
        there = slab.at[pl.ds(pl.multiple_of((1 - y) * 256, 256), 256), pl.ds(columns[slot][0], columns[slot][1])]
        remote(there, there, send_w.at[slot], recv_w.at[slot], me).wait_recv()

    compute(0, 0, 2)
    start_far(0, 0)
    arrived(0)
    compute(1, 0, 2)
    start_far(1, 0)
    for color in range(2):
        compute(color, 0, 1)
        compute(color, 0, 3)
        start_plain(color, 0)
    for color in range(2):
        compute(color, 0, 0)
    for color in range(2):
        relay(color, 0)
    arrived(1)
    compute(0, 1, 2)
    start_far(0, 1)
    compute(0, 1, 1)
    compute(0, 1, 3)
    start_plain(0, 1)
    compute(0, 1, 0)
    arrived(2)
    compute(1, 1, 2)
    start_far(1, 1)
    compute(1, 1, 1)
    compute(1, 1, 3)
    start_plain(1, 1)
    compute(1, 1, 0)
    for color in range(2):
        relay(color, 1)
    for sub in range(2):
        for color in range(2):
            second_stage(color, sub)
    for sub in range(2):
        for color in range(2):
            finish(color, sub)
    for copy in pending:
        copy.wait_send()
    for copy in gathers_z + gathers_x + [gather_y] + rest + over_z + over_x:
        copy.wait_send()
    for step in range(1, 8):
        remote(start.at[spot], start.at[spot], send_0.at[step], recv_0.at[spot], me).wait_send()
    for group in range(4):
        across(group).wait_send()

        @pl.when(group != x)
        def _():
            onward(group).wait_send()


def rotate_and_project(rows, rotations, slab, early):
    bf = jnp.bfloat16
    dma = pltpu.SemaphoreType.DMA
    return pl.pallas_call(
        main_kernel,
        out_shape=jax.ShapeDtypeStruct((32, 8192), bf),
        in_specs=[pl.BlockSpec(memory_space=pltpu.VMEM)] * 2 + [pl.BlockSpec(memory_space=pl.ANY)] * 2,
        out_specs=pl.BlockSpec(memory_space=pltpu.VMEM),
        scratch_shapes=[
            pltpu.VMEM((2, 4, 2, BLK, BLK), bf),
            pltpu.VMEM((2, 4, 2, BLK, BLK), bf),
            pltpu.VMEM((2, 2, 2, BLK, BLK), bf),
            pltpu.VMEM((8, 32, 1024), bf),
            pltpu.VMEM((4, 256, 256), bf),
            pltpu.VMEM((4, 256, 256), bf),
            pltpu.VMEM((4, 256, 256), bf),
            pltpu.VMEM((4, 256, 256), bf),
            pltpu.VMEM((2, 4, 256, 256), bf),
        ]
        + [dma((count,)) for count in (8, 8, 7, 7, 4, 4, 4, 4, 4, 4, 4, 4, 3, 3)]
        + [
            dma,
            pltpu.VMEM((4, 256, 512), bf),
            pltpu.VMEM((512, 4096), bf),
            pltpu.VMEM((2, 2, 4, 2, 256, 512), bf),
            pltpu.VMEM((2, 2, 2, 256, 512), bf),
            pltpu.VMEM((2, 2, 2, 2, 256, 512), bf),
            pltpu.VMEM((2, 2, 4, 2, 32, 1024), bf),
            pltpu.VMEM((2, 2, 8, 32, 1024), bf),
            dma((2, 2, 6)),
            dma((2, 2, 6)),
            dma((2, 2, 8)),
            dma((2, 2, 8)),
            dma,
        ],
        compiler_params=pltpu.CompilerParams(collective_id=1, has_side_effects=True, vmem_limit_bytes=52 * 2**20),
        cost_estimate=pl.CostEstimate(flops=2 * 1024 * 512 * 4096, bytes_accessed=10 * 2**20, transcendentals=0),
    )(rows, rotations, slab, early)


def shards(weight_slab, token_rows, skew_params, pairing):
    side = lax.axis_index("tensor") % 2
    outgoing = lax.dynamic_slice_in_dim(weight_slab, (1 - side) * 4096, 1024, 1)
    early = lax.ppermute(outgoing, "tensor", [(d, d ^ 1) for d in range(32)])
    return rotate_and_project(token_rows, cayley_blocks(skew_params, pairing), weight_slab, early)


def solution(mesh):
    in_specs = (
        P(("layer", "tensor"), None),
        P(("layer", "tensor"), None),
        P("layer", "tensor", None, None),
        P("layer", None),
    )
    out_specs = P(("layer", "tensor"), None)
    return jax.shard_map(shards, mesh=mesh, in_specs=in_specs, out_specs=out_specs, check_vma=False)
```
